512 devices in a mesh: req: 32 (over z, core), hid: 16 (over x, y).
Axes of the slice: x: 4, y: 4, z: 16, core: 2. Of those that a mesh axis runs over, the one named last changes fastest.
Arguments:
- attn_partial: bfloat16 [16, 2048, 2880], P('hid', 'req'), may hold values from -4 to 4
- residual: bfloat16 [2048, 2880], P('req'), may hold values from -6 to 6
- norm_gain: bfloat16 [2880], replicated, may hold values from 0.5 to 1.5
- router_weight: bfloat16 [2880, 32], replicated, may hold values from -0.02734375 to 0.02734375
- router_bias: float32 [32], replicated, may hold values from -2.5 to 2.5
- routes: int32 [2048, 4], P('req'), may hold values from 0 to 31, all different within a row; in each aligned block of 64 rows (0 to 63, 64 to 127, ...) at most 16 rows name the same one
- gate_up: bfloat16 [32, 2880, 5760], P('req', None, 'hid'), may hold values from -0.109375 to 0.109375
- gate_up_bias: bfloat16 [32, 5760], P('req', 'hid'), may hold values from -6 to 6
- down_weight: bfloat16 [32, 2880, 2880], P('req', 'hid'), may hold values from -0.0546875 to 0.0546875
- down_bias: bfloat16 [32, 2880], P('req'), may hold values from -6 to 6
Outputs:
- layer_out: bfloat16 [2048, 2880], P('req')
The draws below stay inside these ranges and needn't reach their ends.
Inputs may be any that keep to these rules, and one draw needn't show every extreme that they name: `routes`: each row names 4 different experts; among the 64 rows of one request group no expert is named by more than 16 rows, and in every draw some expert is named by exactly 16 rows of some group.
All inputs are finite; a program needn't handle non-finite values.
Results may differ from the reference program's by a relative error of at most 0.022.
Values may be sent and summed in bfloat16 or wider, within the bound.
A program may use at most 64 MiB of HBM per device.

```python
import math
import jax
import jax.numpy as jnp
import numpy as np
from jax import lax

D = 2880
FF = 2880
TOP = 4
ROW_GRP = 64
EXPERTS = 32
CAP = 16
ROWS = 2048
N_REQ = 32
N_HID = 16


def block_levels(stream_key, shape, shards, least, top_value):
    level = 1.0
    for axis_at, shards_of in shards:
        draws = jax.random.uniform(jax.random.fold_in(jax.random.fold_in(stream_key, 6), axis_at), (shards_of,), jnp.float32, least / len(shards), top_value / len(shards))
        level = level * jnp.repeat(jnp.exp(draws), shape[axis_at] // shards_of).reshape((-1,) + (1,) * (len(shape) - 1 - axis_at))
    return level


def shared_out(key, own, number, rows, amount, top, most, lean):
    ranking = jax.random.permutation(key, amount)
    packed, usual = load_shares(amount, rows * top, most, lean, True), load_shares(amount, rows * top, most, lean, False)
    places = jnp.arange(amount)

    def named(sizes, offset_by):
        used = int((sizes > 0).sum())
        fixed = max(1, used // 4)
        shifted = fixed + (places - fixed + offset_by * (used - fixed)) % max(1, amount - fixed)
        return jnp.zeros((amount,), jnp.int32).at[ranking[jnp.where(places < fixed, places, shifted)]].set(jnp.asarray(sizes, jnp.int32))

    sizes = jnp.where(number % 4 == 0, named(packed, number // 4), named(usual, number - number // 4 - 1))
    mixed = jax.random.permutation(jax.random.fold_in(own, 3), amount)
    source_of, receiver = mixed[0:amount // 2 * 2:2], mixed[1:amount // 2 * 2:2]
    slack = jnp.minimum(sizes[source_of] - 1, most - sizes[receiver]) // 2
    slack = jnp.where((source_of == ranking[0]) | (receiver == ranking[0]) | (sizes[receiver] == 0), 0, jnp.maximum(slack, 0))
    shifted = jax.random.randint(jax.random.fold_in(own, 4), (amount // 2,), 0, 1 << 20) % (slack + 1)
    sizes = sizes.at[source_of].add(-shifted).at[receiver].add(shifted)
    labels = jnp.searchsorted(jnp.cumsum(sizes), jnp.arange(rows * top), side="right").astype(jnp.int32)
    listing = labels.reshape(top, rows).T
    listing = listing[jax.random.permutation(jax.random.fold_in(own, 1), rows)]
    offset_by = jax.random.randint(jax.random.fold_in(own, 2), (rows, 1), 0, top)
    return jnp.take_along_axis(listing, (jnp.arange(top)[None, :] + offset_by) % top, axis=1)


def load_shares(amount, total, most, skew, full):
    portions = [(1 << 20) // math.isqrt(grade ** skew) + 1 for grade in range(1, amount + 1)]
    largest = most if full else min(most, max(-(-total // amount), total * portions[0] // sum(portions)))
    least = 1 if total - largest >= amount - 1 else 0
    counts, surplus = [largest] + [least] * (amount - 1), total - largest - least * (amount - 1)
    while surplus > 0:
        candidates = [i for i in range(1, amount) if counts[i] < largest] or [i for i in range(1, amount) if counts[i] < most]
        whole, left = sum([portions[i] for i in candidates]), surplus
        for i in candidates:
            more = min(most - counts[i], max(1, left * portions[i] // whole), surplus)
            counts[i] = counts[i] + more
            surplus = surplus - more
    return np.array(counts)


def normal_values(rng, extent, deviation, most, cuts=(), kind=jnp.bfloat16):
    values = jax.random.normal(rng, extent, jnp.float32) * deviation
    if len(cuts) > 0:
        values = block_levels(rng, extent, cuts, -0.22, 0.18) * values
    return jnp.clip(values, min=-most, max=most).astype(kind)


def setup_inputs(seed: int = 0) -> dict:
    splits = jax.random.split(jax.random.key(seed), 11)
    attn_partial = normal_values(splits[0], (N_HID, ROWS, D), 0.25, 4.0, ((0, 16), (1, 32)))
    residual = normal_values(splits[1], (ROWS, D), 1.0, 6.0, ((0, 32),))
    norm_gain = jnp.clip(1.0 + 0.1 * jax.random.normal(splits[2], (D,), jnp.float32), 0.5, 1.5).astype(jnp.bfloat16)
    router_weight = normal_values(splits[3], (D, EXPERTS), (16 * D) ** -0.5, 0.02734375)
    router_bias = normal_values(splits[4], (EXPERTS,), 0.3, 2.5, (), jnp.float32)
    routes_keys = jax.random.split(jax.random.fold_in(splits[5], 1), ROWS // ROW_GRP)
    routes_turns = jax.random.permutation(jax.random.fold_in(splits[5], 3), ROWS // ROW_GRP)
    routes = jax.vmap(lambda own, number: shared_out(jax.random.fold_in(splits[5], 2), own, number, ROW_GRP, EXPERTS, TOP, CAP, 2))(routes_keys, routes_turns).reshape((ROWS, TOP))
    gate_up = normal_values(splits[6], (EXPERTS, D, 2 * FF), D ** -0.5, 0.109375, ((0, 32), (2, 16)))
    gate_up_bias = normal_values(splits[7], (EXPERTS, 2 * FF), 1.5, 6.0, ((0, 32), (1, 16)))
    down_weight = normal_values(splits[8], (EXPERTS, FF, D), (4 * FF) ** -0.5, 0.0546875, ((0, 32), (1, 16)))
    down_bias = normal_values(splits[9], (EXPERTS, D), 0.5, 6.0, ((0, 32),))
    return dict(attn_partial=attn_partial, residual=residual, norm_gain=norm_gain, router_weight=router_weight, router_bias=router_bias, routes=routes, gate_up=gate_up, gate_up_bias=gate_up_bias, down_weight=down_weight, down_bias=down_bias)


def expert_apply(inputs, gate_up, gate_up_bias, down_weight, down_bias):
    preact = jnp.dot(inputs, gate_up, preferred_element_type=jnp.float32) + gate_up_bias.astype(jnp.float32)
    gate_part = jnp.minimum(preact[:, 0::2], 7.0)
    up_part = jnp.clip(preact[:, 1::2], -7.0, 7.0)
    activated = ((up_part + 1.0) * gate_part * jax.nn.sigmoid(1.702 * gate_part)).astype(jnp.bfloat16)
    blocks = activated.reshape(inputs.shape[0], N_HID, FF // N_HID).astype(jnp.float32)
    down_blocks = down_weight.reshape(N_HID, FF // N_HID, D).astype(jnp.float32)
    partial_value = jnp.einsum('rhf,hfd->hrd', blocks, down_blocks).astype(jnp.bfloat16)
    summed = lax.optimization_barrier(jnp.sum(partial_value.astype(jnp.float32), axis=0)) + down_bias.astype(jnp.float32)
    return summed.astype(jnp.bfloat16)

def slot_numbers(routes):
    pair_ids = routes.reshape(N_REQ, ROW_GRP * TOP)
    onehot = (pair_ids[:, :, None] == jnp.arange(EXPERTS, dtype=jnp.int32)[None, None, :]).astype(jnp.int32)
    before = jnp.cumsum(onehot, axis=1).astype(jnp.int32) - onehot
    return lax.optimization_barrier(jnp.sum(before * onehot, axis=2)).astype(jnp.int32)

def reference(attn_partial, residual, norm_gain, router_weight, router_bias, routes, gate_up, gate_up_bias, down_weight, down_bias):
    attention = lax.optimization_barrier(jnp.sum(attn_partial.astype(jnp.float32), axis=0))
    stream = (residual.astype(jnp.float32) + attention).astype(jnp.bfloat16)
    widened = stream.astype(jnp.float32)
    inverse = lax.rsqrt(lax.optimization_barrier(jnp.mean(widened * widened, axis=1, keepdims=True)) + 1e-05)
    normed = (widened * inverse * norm_gain.astype(jnp.float32)).astype(jnp.bfloat16)
    logits = jnp.dot(normed, router_weight, preferred_element_type=jnp.float32) + router_bias.astype(jnp.float32)
    picked = jnp.take_along_axis(logits, routes, axis=1)
    raised = jnp.exp(picked)
    combine = (raised / lax.optimization_barrier(jnp.sum(raised, axis=1, keepdims=True))).astype(jnp.bfloat16)
    slot_ids = slot_numbers(routes).reshape(ROWS, TOP)
    groups = (jnp.arange(ROWS, dtype=jnp.int32) // ROW_GRP)[:, None]
    target = (routes * (N_REQ * CAP) + groups * CAP + slot_ids).astype(jnp.int32).reshape(ROWS * TOP)
    sources = jnp.broadcast_to(normed[:, None, :], (ROWS, TOP, D)).reshape(ROWS * TOP, D)
    flat_rows = jnp.zeros((EXPERTS * N_REQ * CAP, D), jnp.bfloat16).at[target].set(sources)
    buffer = flat_rows.reshape(EXPERTS, N_REQ * CAP, D)
    outputs = lax.map(lambda operands: expert_apply(*operands), (buffer, gate_up, gate_up_bias, down_weight, down_bias))
    chosen = outputs.reshape(EXPERTS * N_REQ * CAP, D)[target].reshape(ROWS, TOP, D).astype(jnp.float32)
    mixture = lax.optimization_barrier(jnp.sum(chosen * combine.astype(jnp.float32)[:, :, None], axis=1))
    return (widened + mixture).astype(jnp.bfloat16)
```

```python
import functools

import jax
import jax.numpy as jnp
from jax import lax
from jax.experimental import pallas as pl
from jax.experimental.pallas import tpu as pltpu
from jax.sharding import PartitionSpec as P

MESH = pl.DeviceIdType.MESH
BLK = 384
NBLK = 8
SLOTS = 8
BF = jnp.bfloat16
F32 = jnp.float32


def lanes(block):
    return pl.ds(pl.multiple_of(block * BLK, 128), BLK)


def moe_kernel(
    n_req,
    n_hid,
    attn_ref,
    resid_ref,
    gain_ref,
    wr_ref,
    rb_ref,
    routes_ref,
    bgu_ref,
    db_ref,
    wgu_hbm,
    wd_hbm,
    out_ref,
    attn_s,
    resid_s,
    gain_s,
    wr_s,
    db_s,
    wgu_v,
    wd_v,
    wg_s,
    wd_s,
    r1,
    stat_s,
    rstat,
    zout,
    zin,
    ag,
    acc,
    ssq,
    act_s,
    pout,
    rs,
    zbout,
    zbin,
    fin_s,
    rfin,
    w_sem,
    s1,
    q1,
    s2,
    q2,
    s3,
    q3,
    s4,
    q4,
    s5,
    q5,
    s6,
    q6,
    s7,
    q7,
):
    rows, width = attn_ref.shape
    experts = rb_ref.shape[1]
    half = wd_hbm.shape[0]
    wide = BLK * NBLK
    tail = wide - 256
    h = lax.axis_index("hid")
    g = lax.axis_index("req")
    sg = lax.div(h, NBLK)
    f = lax.rem(h, NBLK)

    get_wgu = pltpu.make_async_copy(wgu_hbm, wgu_v, w_sem.at[0])
    get_wd = pltpu.make_async_copy(wd_hbm, wd_v, w_sem.at[1])
    get_wgu.start()
    get_wd.start()

    barrier = pltpu.get_barrier_semaphore()

    @pl.loop(1, n_hid)
    def _(d):
        pl.semaphore_signal(
            barrier, inc=1, device_id={"hid": lax.rem(h + d, n_hid)}, device_id_type=MESH
        )

    @pl.loop(1, n_req)
    def _(d):
        pl.semaphore_signal(
            barrier, inc=1, device_id={"req": lax.rem(g + d, n_req)}, device_id_type=MESH
        )

    attn_s[:, tail:] = jnp.zeros((rows, wide - tail), BF)
    attn_s[:, :width] = attn_ref[...]
    resid_s[:, tail:] = jnp.zeros((rows, wide - tail), BF)
    resid_s[:, :width] = resid_ref[...]
    gain_s[:, tail:] = jnp.zeros((1, wide - tail), F32)
    gain_s[:, :width] = gain_ref[...].astype(F32)
    db_s[:, tail:] = jnp.zeros((1, wide - tail), F32)
    db_s[:, :width] = db_ref[...].astype(F32)

    pl.semaphore_wait(barrier, n_hid + n_req - 2)

    def hid_copy(src, dst, send, recv, peer):
        return pltpu.make_async_remote_copy(
            src_ref=src,
            dst_ref=dst,
            send_sem=send,
            recv_sem=recv,
            device_id={"hid": peer},
            device_id_type=MESH,
        )

    def req_copy(src, dst, send, recv, peer):
        return pltpu.make_async_remote_copy(
            src_ref=src,
            dst_ref=dst,
            send_sem=send,
            recv_sem=recv,
            device_id={"req": peer},
            device_id_type=MESH,
        )

    @pl.loop(1, n_hid)
    def _(d):
        p = lax.rem(h + d, n_hid)
        src = attn_s.at[:, lanes(lax.rem(p, NBLK))]
        hid_copy(src, r1.at[h], s1.at[p], q1.at[h], p).start()

    wr_s[pl.ds(width, wide - width), :] = jnp.zeros((wide - width, 128), BF)
    spread = (
        lax.broadcasted_iota(jnp.int32, (experts, 128), 0)
        == lax.broadcasted_iota(jnp.int32, (experts, 128), 1)
    ).astype(BF)
    wr_s[pl.ds(0, width), :] = jnp.dot(
        wr_ref[...], spread, preferred_element_type=F32
    ).astype(BF)
    named = lax.broadcasted_iota(jnp.int32, (rows, experts), 1)
    mask = jnp.zeros((rows, experts), F32)
    for k in range(routes_ref.shape[1]):
        mask = mask + jnp.where(routes_ref[:, k : k + 1] == named, 1.0, 0.0)
    earlier = (
        lax.broadcasted_iota(jnp.int32, (rows, rows), 1)
        < lax.broadcasted_iota(jnp.int32, (rows, rows), 0)
    ).astype(BF)
    slot = jnp.dot(earlier, mask.astype(BF), preferred_element_type=F32)
    pairs = experts * SLOTS
    col = lax.broadcasted_iota(jnp.int32, (experts, pairs), 1)
    own = lax.broadcasted_iota(jnp.int32, (experts, pairs), 0)
    expand = (lax.div(col, SLOTS) == own).astype(BF)
    slot_wide = jnp.dot(slot.astype(BF), expand, preferred_element_type=F32)
    mask_wide = jnp.dot(mask.astype(BF), expand, preferred_element_type=F32)
    want = lax.rem(lax.broadcasted_iota(jnp.int32, (rows, pairs), 1), SLOTS) + sg * SLOTS
    chosen = jnp.where((slot_wide == want.astype(F32)) & (mask_wide > 0.5), 1.0, 0.0)

    def add1(d, total):
        p = lax.rem(h - d + n_hid, n_hid)
        hid_copy(r1.at[p], r1.at[p], s1.at[p], q1.at[p], p).wait_recv()
        return total + r1[p].astype(F32)

    attention = lax.fori_loop(1, n_hid, add1, attn_s[:, lanes(f)].astype(F32))
    stream = (resid_s[:, lanes(f)].astype(F32) + attention).astype(BF)
    stream_wide = stream.astype(F32)

    picked = lax.dot_general(
        chosen.astype(BF), stream, (((0,), (0,)), ((), ())), preferred_element_type=F32
    )
    zout[...] = picked.reshape(experts, SLOTS, BLK).astype(BF)

    @pl.loop(1, n_req)
    def _(d):
        p = lax.rem(g + d, n_req)
        req_copy(zout.at[p], zin.at[g], s2.at[p], q2.at[g], p).start()

    scaled = (stream_wide * gain_s[:, lanes(f)]).astype(BF)
    stats = jnp.dot(
        scaled, wr_s[pl.ds(pl.multiple_of(f * BLK, 128), BLK), :], preferred_element_type=F32
    )
    squares = jnp.sum(stream_wide * stream_wide, axis=1, keepdims=True)
    lane = lax.broadcasted_iota(jnp.int32, (rows, 128), 1)
    stat_s[...] = jnp.where(lane == experts, squares, stats)

    @pl.loop(1, NBLK)
    def _(d):
        pf = lax.rem(f + d, NBLK)
        hid_copy(
            stat_s, rstat.at[f], s3.at[pf], q3.at[f], sg * NBLK + pf
        ).start()

    get_wgu.wait()
    twice = wgu_v.shape[1]
    from_col = lax.broadcasted_iota(jnp.int32, (twice, 512), 0)
    to_col = lax.broadcasted_iota(jnp.int32, (twice, 512), 1)
    perm = (to_col == lax.rem(from_col, 2) * 256 + lax.div(from_col, 2)).astype(BF)

    @pl.loop(0, width // 192)
    def _(i):
        at = pl.ds(pl.multiple_of(i * 192, 64), 192)
        wg_s[at, :] = jnp.dot(wgu_v[at, :], perm, preferred_element_type=F32).astype(BF)

    wg_s[pl.ds(width, wide - width), :] = jnp.zeros((wide - width, 512), BF)
    bias = jnp.dot(
        jnp.broadcast_to(bgu_ref[...], (16, twice)), perm, preferred_element_type=F32
    )[0:1, :]
    get_wd.wait()
    wd_s[...] = jnp.zeros(wd_s.shape, BF)
    wd_s[0:half, 0:width] = wd_v[...]
    acc[...] = jnp.zeros(acc.shape, F32)
    ssq[...] = jnp.zeros(ssq.shape, F32)

    zin[g] = zout[g]

    @pl.loop(1, n_req)
    def _(d):
        p = lax.rem(g - d + n_req, n_req)
        req_copy(zin.at[p], zin.at[p], s2.at[p], q2.at[p], p).wait_recv()

    @pl.loop(1, n_hid)
    def _(d):
        p = lax.rem(h + d, n_hid)
        hid_copy(zin, ag.at[h], s4.at[p], q4.at[h], p).start()

    def use_block(block, at):
        wide_rows = block.astype(F32).reshape(n_req * SLOTS, BLK)
        side = lax.div(at, NBLK)
        blk = lax.rem(at, NBLK)
        sq = wide_rows * wide_rows
        ssq[side] += sq[:, 0:128] + sq[:, 128:256] + sq[:, 256:384]
        u = (wide_rows * gain_s[:, lanes(blk)]).astype(BF)
        w = wg_s[pl.ds(pl.multiple_of(blk * BLK, 128), BLK), :]
        acc[side] += jnp.dot(u, w, preferred_element_type=F32)

    use_block(zin[...], h)

    @pl.loop(1, n_hid)
    def _(d):
        p = lax.rem(h - d + n_hid, n_hid)
        hid_copy(ag.at[p], ag.at[p], s4.at[p], q4.at[p], p).wait_recv()
        use_block(ag[p], p)

    for side in range(2):
        mean = jnp.sum(ssq[side], axis=1, keepdims=True) * (1.0 / width)
        inverse = lax.rsqrt(mean + 1e-05)
        gate = jnp.minimum(acc[side, :, 0:256] * inverse + bias[:, 0:256], 7.0)
        up = jnp.clip(acc[side, :, 256:512] * inverse + bias[:, 256:512], -7.0, 7.0)
        act_s[side] = ((up + 1.0) * gate * jax.nn.sigmoid(1.702 * gate)).astype(BF)

    def down(p):
        return jnp.dot(
            act_s[lax.div(p, NBLK)], wd_s[:, lanes(lax.rem(p, NBLK))], preferred_element_type=F32
        ).astype(BF)

    @pl.loop(1, n_hid)
    def _(d):
        p = lax.rem(h + d, n_hid)
        pout[p] = down(p)
        hid_copy(pout.at[p], rs.at[h], s5.at[p], q5.at[h], p).start()

    total_stats = stat_s[...]
    for d in range(1, NBLK):
        pf = lax.rem(f - d + NBLK, NBLK)
        hid_copy(rstat.at[pf], rstat.at[pf], s3.at[pf], q3.at[pf], sg * NBLK + pf).wait_recv()
        total_stats = total_stats + rstat[pf]
    row_sq = jnp.sum(jnp.where(lane == experts, total_stats, 0.0), axis=1, keepdims=True)
    row_inverse = lax.rsqrt(row_sq * (1.0 / width) + 1e-05)
    logits = total_stats[:, 0:experts] * row_inverse + rb_ref[...]
    raised = jnp.where(mask > 0.5, jnp.exp(jnp.where(mask > 0.5, logits, 0.0)), 0.0)
    combine = (raised / jnp.sum(raised, axis=1, keepdims=True)).astype(BF)
    combine_wide = jnp.dot(combine, expand, preferred_element_type=F32)
    weights = jnp.where(chosen > 0.5, combine_wide, 0.0).astype(BF)

    def add5(d, total):
        p = lax.rem(h - d + n_hid, n_hid)
        hid_copy(rs.at[p], rs.at[p], s5.at[p], q5.at[p], p).wait_recv()
        return total + rs[p].astype(F32)

    summed = lax.fori_loop(1, n_hid, add5, down(h).astype(F32))
    expert_out = summed + db_s[:, lanes(f)]

    zbout[...] = expert_out.reshape(n_req, SLOTS, BLK).astype(BF)

    @pl.loop(1, n_req)
    def _(d):
        p = lax.rem(g + d, n_req)
        req_copy(zbout.at[p], zbin.at[g], s6.at[p], q6.at[g], p).start()

    zbin[g] = zbout[g]

    @pl.loop(1, n_req)
    def _(d):
        p = lax.rem(g - d + n_req, n_req)
        req_copy(zbin.at[p], zbin.at[p], s6.at[p], q6.at[p], p).wait_recv()

    returned = zbin[...].astype(F32).reshape(pairs, BLK).astype(BF)
    mixture = jnp.dot(weights, returned, preferred_element_type=F32)
    first = jnp.where(sg == 0, 1.0, 0.0)
    fin_s[...] = (mixture + stream_wide * first).astype(BF)

    @pl.loop(1, n_hid)
    def _(d):
        p = lax.rem(h + d, n_hid)
        hid_copy(fin_s, rfin.at[h], s7.at[p], q7.at[h], p).start()

    rfin[h] = fin_s[...]

    @pl.loop(1, n_hid)
    def _(d):
        p = lax.rem(h - d + n_hid, n_hid)
        hid_copy(rfin.at[p], rfin.at[p], s7.at[p], q7.at[p], p).wait_recv()

    for b in range(NBLK):
        size = min(BLK, width - b * BLK)
        both = rfin[b].astype(F32) + rfin[NBLK + b].astype(F32)
        out_ref[:, b * BLK : b * BLK + size] = both[:, :size].astype(BF)

    @pl.loop(1, n_hid)
    def _(d):
        p = lax.rem(h + d, n_hid)
        hid_copy(r1.at[p], r1.at[p], s1.at[p], q1.at[p], p).wait_send()
        hid_copy(zin, ag.at[p], s4.at[p], q4.at[p], p).wait_send()
        hid_copy(rs.at[p], rs.at[p], s5.at[p], q5.at[p], p).wait_send()
        hid_copy(fin_s, rfin.at[p], s7.at[p], q7.at[p], p).wait_send()

    @pl.loop(1, NBLK)
    def _(d):
        pf = lax.rem(f + d, NBLK)
        hid_copy(stat_s, rstat.at[pf], s3.at[pf], q3.at[pf], sg * NBLK + pf).wait_send()

    @pl.loop(1, n_req)
    def _(d):
        p = lax.rem(g + d, n_req)
        req_copy(zout.at[p], zin.at[p], s2.at[p], q2.at[p], p).wait_send()
        req_copy(zbout.at[p], zbin.at[p], s6.at[p], q6.at[p], p).wait_send()


def on_device(
    attn_partial,
    residual,
    norm_gain,
    router_weight,
    router_bias,
    routes,
    gate_up,
    gate_up_bias,
    down_weight,
    down_bias,
):
    n_req, n_hid = lax.axis_size("req"), lax.axis_size("hid")
    rows, width = residual.shape
    wide = BLK * NBLK
    per = n_req * SLOTS
    vmem = pl.BlockSpec(memory_space=pltpu.VMEM)
    hbm = pl.BlockSpec(memory_space=pl.ANY)
    dma = pltpu.SemaphoreType.DMA
    hid_sem, req_sem = dma((n_hid,)), dma((n_req,))
    return pl.pallas_call(
        functools.partial(moe_kernel, n_req, n_hid),
        out_shape=jax.ShapeDtypeStruct((rows, width), BF),
        in_specs=[vmem] * 8 + [hbm] * 2,
        out_specs=vmem,
        scratch_shapes=[
            pltpu.VMEM((rows, wide), BF),
            pltpu.VMEM((rows, wide), BF),
            pltpu.VMEM((1, wide), F32),
            pltpu.VMEM((wide, 128), BF),
            pltpu.VMEM((1, wide), F32),
            pltpu.VMEM(gate_up.shape[1:], BF),
            pltpu.VMEM(down_weight.shape[1:], BF),
            pltpu.VMEM((wide, 512), BF),
            pltpu.VMEM((256, wide), BF),
            pltpu.VMEM((n_hid, rows, BLK), BF),
            pltpu.VMEM((rows, 128), F32),
            pltpu.VMEM((NBLK, rows, 128), F32),
            pltpu.VMEM((n_req, SLOTS, BLK), BF),
            pltpu.VMEM((n_req, SLOTS, BLK), BF),
            pltpu.VMEM((n_hid, n_req, SLOTS, BLK), BF),
            pltpu.VMEM((2, per, 512), F32),
            pltpu.VMEM((2, per, 128), F32),
            pltpu.VMEM((2, per, 256), BF),
            pltpu.VMEM((n_hid, per, BLK), BF),
            pltpu.VMEM((n_hid, per, BLK), BF),
            pltpu.VMEM((n_req, SLOTS, BLK), BF),
            pltpu.VMEM((n_req, SLOTS, BLK), BF),
            pltpu.VMEM((rows, BLK), BF),
            pltpu.VMEM((n_hid, rows, BLK), BF),
            dma((2,)),
            hid_sem,
            hid_sem,
            req_sem,
            req_sem,
            dma((NBLK,)),
            dma((NBLK,)),
            hid_sem,
            hid_sem,
            hid_sem,
            hid_sem,
            req_sem,
            req_sem,
            hid_sem,
            hid_sem,
        ],
        compiler_params=pltpu.CompilerParams(
            collective_id=0, has_side_effects=True, vmem_limit_bytes=56 * 1024 * 1024
        ),
        name="moe_block",
    )(
        attn_partial[0],
        residual,
        norm_gain.reshape(1, width),
        router_weight,
        router_bias.reshape(1, -1),
        routes,
        gate_up_bias,
        down_bias,
        gate_up[0],
        down_weight[0],
    )


def solution(mesh):
    return jax.shard_map(
        on_device,
        mesh=mesh,
        in_specs=(
            P("hid", "req", None),
            P("req", None),
            P(),
            P(),
            P(),
            P("req", None),
            P("req", None, "hid"),
            P("req", "hid"),
            P("req", "hid", None),
            P("req", None),
        ),
        out_specs=P("req", None),
        check_vma=False,
    )
```

```python
import functools

import jax
import jax.numpy as jnp
from jax import lax
from jax.experimental import pallas as pl
from jax.experimental.pallas import tpu as pltpu
from jax.sharding import PartitionSpec as P

MESH = pl.DeviceIdType.MESH
BLK = 384
NBLK = 8
SLOTS = 8
BF = jnp.bfloat16
F32 = jnp.float32


def lanes(block):
    return pl.ds(pl.multiple_of(block * BLK, 128), BLK)


def dot_nt(left, right):
    return lax.dot_general(
        left, right, (((1,), (1,)), ((), ())), preferred_element_type=F32
    )


def moe_kernel(
    n_req,
    n_hid,
    attn_ref,
    resid_ref,
    gain_ref,
    wr_ref,
    rb_ref,
    routes_ref,
    bgu_ref,
    db_ref,
    wgu_hbm,
    wd_hbm,
    out_ref,
    attn_s,
    resid_s,
    gain_s,
    wr_s,
    db_s,
    wgu_v,
    wd_v,
    wg_s,
    wd_s,
    r1,
    stat_s,
    rstat,
    zout,
    ag,
    acc,
    ssq,
    act_s,
    pout,
    tot,
    rb1,
    rb2,
    ra1,
    ra2,
    zbout,
    zbin,
    fin_s,
    rfin,
    w_sem,
    s1,
    q1,
    s2,
    q2,
    s3,
    q3,
    s4,
    q4,
    s5,
    q5,
    s6,
    q6,
    s7,
    q7,
):
    rows, width = attn_ref.shape
    experts = rb_ref.shape[1]
    half = wd_hbm.shape[0]
    wide = BLK * NBLK
    tail = wide - 256
    h = lax.axis_index("hid")
    g = lax.axis_index("req")
    sg = lax.div(h, NBLK)
    f = lax.rem(h, NBLK)

    get_wgu = pltpu.make_async_copy(wgu_hbm, wgu_v, w_sem.at[0])
    get_wd = pltpu.make_async_copy(wd_hbm, wd_v, w_sem.at[1])
    get_wgu.start()
    get_wd.start()

    barrier = pltpu.get_barrier_semaphore()

    @pl.loop(1, n_hid)
    def _(d):
        pl.semaphore_signal(
            barrier, inc=1, device_id={"hid": lax.rem(h + d, n_hid)}, device_id_type=MESH
        )

    @pl.loop(1, n_req)
    def _(d):
        pl.semaphore_signal(
            barrier, inc=1, device_id={"req": lax.rem(g + d, n_req)}, device_id_type=MESH
        )

    attn_s[:, tail:] = jnp.zeros((rows, wide - tail), BF)
    attn_s[:, :width] = attn_ref[...]
    resid_s[:, tail:] = jnp.zeros((rows, wide - tail), BF)
    resid_s[:, :width] = resid_ref[...]
    gain_s[:, tail:] = jnp.zeros((1, wide - tail), F32)
    gain_s[:, :width] = gain_ref[...].astype(F32)
    db_s[:, tail:] = jnp.zeros((1, wide - tail), F32)
    db_s[:, :width] = db_ref[...].astype(F32)

    pl.semaphore_wait(barrier, n_hid + n_req - 2)

    def hid_copy(src, dst, send, recv, peer):
        return pltpu.make_async_remote_copy(
            src_ref=src,
            dst_ref=dst,
            send_sem=send,
            recv_sem=recv,
            device_id={"hid": peer},
            device_id_type=MESH,
        )

    def req_copy(src, dst, send, recv, peer):
        return pltpu.make_async_remote_copy(
            src_ref=src,
            dst_ref=dst,
            send_sem=send,
            recv_sem=recv,
            device_id={"req": peer},
            device_id_type=MESH,
        )

    @pl.loop(1, n_hid)
    def _(d):
        p = lax.rem(h + d, n_hid)
        src = attn_s.at[:, lanes(lax.rem(p, NBLK))]
        hid_copy(src, r1.at[h], s1.at[p], q1.at[h], p).start()

    wr_s[...] = jnp.zeros(wr_s.shape, BF)
    wr_s[0:experts, 0:width] = wr_ref[...]
    named = lax.broadcasted_iota(jnp.int32, (experts, rows), 0)
    mask_t = jnp.zeros((experts, rows), F32)
    for k in range(routes_ref.shape[0]):
        mask_t = mask_t + jnp.where(routes_ref[k : k + 1, :] == named, 1.0, 0.0)
    row_a = lax.broadcasted_iota(jnp.int32, (rows, rows), 0)
    row_b = lax.broadcasted_iota(jnp.int32, (rows, rows), 1)
    same = (row_a == row_b).astype(BF)
    mask_t = mask_t.astype(BF)
    slot_t = jnp.dot(mask_t, (row_a < row_b).astype(BF), preferred_element_type=F32)
    pairs = experts * SLOTS
    col = lax.broadcasted_iota(jnp.int32, (pairs, experts), 0)
    own = lax.broadcasted_iota(jnp.int32, (pairs, experts), 1)
    expand_t = (lax.div(col, SLOTS) == own).astype(BF)
    slot_wide = jnp.dot(expand_t, slot_t.astype(BF), preferred_element_type=F32)
    mask_wide = jnp.dot(expand_t, mask_t, preferred_element_type=F32)
    want = lax.rem(lax.broadcasted_iota(jnp.int32, (pairs, rows), 0), SLOTS) + sg * SLOTS
    chosen_t = jnp.where((slot_wide == want.astype(F32)) & (mask_wide > 0.5), 1.0, 0.0)
    chosen_t = chosen_t.astype(BF)
    chosen = dot_nt(same, chosen_t)
    mask = dot_nt(same, mask_t)

    def add1(d, total):
        p = lax.rem(h - d + n_hid, n_hid)
        hid_copy(r1.at[p], r1.at[p], s1.at[p], q1.at[p], p).wait_recv()
        return total + r1[p].astype(F32)

    attention = lax.fori_loop(1, n_hid, add1, attn_s[:, lanes(f)].astype(F32))
    stream = (resid_s[:, lanes(f)].astype(F32) + attention).astype(BF)
    stream_wide = stream.astype(F32)

    picked = jnp.dot(chosen_t, stream, preferred_element_type=F32)
    zout[...] = picked.reshape(experts, SLOTS, BLK).astype(BF)

    @pl.loop(1, n_req)
    def _(d):
        p = lax.rem(g + d, n_req)
        req_copy(zout.at[p], ag.at[h, g], s2.at[p], q2.at[g], p).start()

    scaled = (stream_wide * gain_s[:, lanes(f)]).astype(BF)
    stats = dot_nt(scaled, wr_s[:, lanes(f)])
    squares = jnp.sum(stream_wide * stream_wide, axis=1, keepdims=True)
    lane = lax.broadcasted_iota(jnp.int32, (rows, 128), 1)
    stat_s[...] = jnp.where(lane == experts, squares, stats)

    @pl.loop(1, NBLK)
    def _(d):
        pf = lax.rem(f + d, NBLK)
        hid_copy(
            stat_s, rstat.at[f], s3.at[pf], q3.at[f], sg * NBLK + pf
        ).start()

    get_wgu.wait()
    twice = wgu_v.shape[0]
    from_col = lax.broadcasted_iota(jnp.int32, (512, twice), 1)
    to_col = lax.broadcasted_iota(jnp.int32, (512, twice), 0)
    perm = (to_col == lax.rem(from_col, 2) * 256 + lax.div(from_col, 2)).astype(BF)
    wg_s[:, tail:] = jnp.zeros((512, wide - tail), BF)

    @pl.loop(0, width // BLK)
    def _(i):
        at = lanes(i)
        wg_s[:, at] = jnp.dot(perm, wgu_v[:, at], preferred_element_type=F32).astype(BF)

    last = width // BLK * BLK
    wg_s[:, last:width] = jnp.dot(
        perm, wgu_v[:, last:width], preferred_element_type=F32
    ).astype(BF)
    bias = dot_nt(jnp.broadcast_to(bgu_ref[...], (16, twice)), perm)[0:1, :]
    get_wd.wait()
    wd_s[...] = jnp.zeros(wd_s.shape, BF)
    wd_s[0:half, 0:width] = wd_v[...]
    acc[...] = jnp.zeros(acc.shape, F32)
    ssq[...] = jnp.zeros(ssq.shape, F32)

    side = 4
    x = lax.div(h, side)
    y = lax.rem(h, side)

    def at(c, da, db):
        a = lax.rem((x if c == 0 else y) + da, side)
        b = lax.rem((y if c == 0 else x) + db, side)
        return a * side + b if c == 0 else b * side + a

    quart = n_req // 4

    def piece(p, q):
        return ag.at[p, pl.ds(q * quart, quart)]

    def ship(q, k, p, peer):
        hid_copy(piece(p, q), piece(p, q), s4.at[q, k], q4.at[p, q], peer).start()

    def arrive(q, p):
        hid_copy(piece(p, q), piece(p, q), s4.at[q, 0], q4.at[p, q], p).wait_recv()

    def use_half(p, c):
        wide_rows = ag[p, c * 2 * quart : (c + 1) * 2 * quart].astype(F32)
        count = 2 * quart * SLOTS
        wide_rows = wide_rows.reshape(count, BLK)
        to = lax.div(p, NBLK)
        blk = lax.rem(p, NBLK)
        sq = wide_rows * wide_rows
        here = slice(c * count, (c + 1) * count)
        ssq[to, here] += sq[:, 0:128] + sq[:, 128:256] + sq[:, 256:384]
        u = (wide_rows * gain_s[:, lanes(blk)]).astype(BF)
        acc[to, here] += dot_nt(u, wg_s[:, lanes(blk)])

    ag[h, g] = zout[g]
    for q in range(4):
        c = q // 2

        @pl.loop(q * quart, (q + 1) * quart)
        def _(p):
            @pl.when(p != g)
            def _():
                req_copy(zout.at[p], ag.at[h, p], s2.at[p], q2.at[p], p).wait_recv()

        ship(q, 0, h, at(c, 1, 0))
        ship(q, 1, h, at(c, 3, 0))
        ship(q, 3, h, at(c, 0, 1))
        ship(q, 4, h, at(c, 0, 3))
    for c in range(2):
        use_half(h, c)
    for q in range(4):
        c, odd = q // 2, q % 2
        arrive(q, at(c, 1, 0))
        arrive(q, at(c, 3, 0))
        if odd:
            ship(q, 2, at(c, 1, 0), at(c, 3, 0))
        else:
            ship(q, 2, at(c, 3, 0), at(c, 1, 0))
        for j in (1, 3):
            ship(q, 3 + 2 * j, at(c, j, 0), at(c, 0, 1))
            ship(q, 4 + 2 * j, at(c, j, 0), at(c, 0, 3))
    for c in range(2):

        @pl.loop(0, 2)
        def _(i):
            use_half(at(c, 2 * i + 1, 0), c)

    for q in range(4):
        c = q // 2
        arrive(q, at(c, 2, 0))
        ship(q, 7, at(c, 2, 0), at(c, 0, 1))
        ship(q, 8, at(c, 2, 0), at(c, 0, 3))

    @pl.loop(0, 4)
    def _(i):
        j = lax.rem(i + i + i, 4)
        for q in range(4):
            c, odd = q // 2, q % 2
            arrive(q, at(c, j, 1))
            arrive(q, at(c, j, 3))
            if odd:
                ship(q, 11 + j, at(c, j, 1), at(c, 0, 3))
            else:
                ship(q, 11 + j, at(c, j, 3), at(c, 0, 1))

    for c in range(2):
        use_half(at(c, 2, 0), c)

        @pl.loop(0, 4)
        def _(j):
            use_half(at(c, j, 1), c)
            use_half(at(c, j, 3), c)

    @pl.loop(0, 4)
    def _(i):
        j = lax.rem(i + i + i, 4)
        for q in range(4):
            arrive(q, at(q // 2, j, 2))
        for c in range(2):
            use_half(at(c, j, 2), c)

    for side_at in range(2):
        mean = jnp.sum(ssq[side_at], axis=1, keepdims=True) * (1.0 / width)
        inverse = lax.rsqrt(mean + 1e-05)
        gate = jnp.minimum(acc[side_at, :, 0:256] * inverse + bias[:, 0:256], 7.0)
        up = jnp.clip(acc[side_at, :, 256:512] * inverse + bias[:, 256:512], -7.0, 7.0)
        act_s[side_at] = ((up + 1.0) * gate * jax.nn.sigmoid(1.702 * gate)).astype(BF)

    rowq = quart * SLOTS

    def down(p, c):
        here = slice(c * 2 * rowq, (c + 1) * 2 * rowq)
        pout[p, here] = jnp.dot(
            act_s[lax.div(p, NBLK), here],
            wd_s[:, lanes(lax.rem(p, NBLK))],
            preferred_element_type=F32,
        ).astype(BF)

    def part(p, q):
        return pout.at[p, pl.ds(q * rowq, rowq)]

    def load(p, q):
        return pout[p, pl.ds(q * rowq, rowq)].astype(F32)

    def pass_on(q, k, m, p, dst, peer):
        hid_copy(part(p, q), dst, s5.at[q, k], q5.at[q, m], peer).start()

    def landed(q, m, dst):
        hid_copy(dst, dst, s5.at[q, 0], q5.at[q, m], at(0, 1, 0)).wait_recv()

    @pl.loop(0, 4)
    def _(j):
        for c in range(2):
            down(at(c, j, 2), c)
        for q in range(4):
            c, odd = q // 2, q % 2
            peer = at(c, 0, 1) if odd else at(c, 0, 3)
            pass_on(q, j, j, at(c, j, 2), rb1.at[q, j], peer)

    @pl.loop(0, 4)
    def _(j):
        for c in range(2):
            down(at(c, j, 1), c)
            down(at(c, j, 3), c)
        for q in range(4):
            c, odd = q // 2, q % 2
            to = 3 if odd else 1
            pass_on(q, 4 + j, 4 + j, at(c, j, to), rb2.at[q, j, 0], at(c, 0, to))

    @pl.loop(0, 4)
    def _(j):
        for q in range(4):
            c, odd = q // 2, q % 2
            to = 1 if odd else 3
            p = at(c, j, to)
            landed(q, j, rb1.at[q, j])
            both = load(p, q) + rb1[q, j].astype(F32)
            pout[p, pl.ds(q * rowq, rowq)] = both.astype(BF)
            pass_on(q, 8 + j, 8 + j, p, rb2.at[q, j, 1], at(c, 0, to))
        for c in range(2):
            down(at(c, j, 0), c)

    def line_sum(j, q):
        landed(q, 4 + j, rb2.at[q, j, 0])
        landed(q, 8 + j, rb2.at[q, j, 1])
        p = at(q // 2, j, 0)
        both = load(p, q) + rb2[q, j, 0].astype(F32) + rb2[q, j, 1].astype(F32)
        pout[p, pl.ds(q * rowq, rowq)] = both.astype(BF)
        return both

    for q in range(4):
        c, odd = q // 2, q % 2
        line_sum(2, q)
        pass_on(q, 12, 12, at(c, 2, 0), ra1.at[q], at(c, 1 if odd else 3, 0))
    for q in range(4):
        c, odd = q // 2, q % 2
        to = 3 if odd else 1
        line_sum(to, q)
        pass_on(q, 13, 13, at(c, to, 0), ra2.at[q, 0], at(c, to, 0))
    for q in range(4):
        line_sum(1 if q % 2 else 3, q)
        tot[q * rowq : (q + 1) * rowq] = line_sum(0, q)
    for q in range(4):
        c, odd = q // 2, q % 2
        to = 1 if odd else 3
        p = at(c, to, 0)
        landed(q, 12, ra1.at[q])
        both = load(p, q) + ra1[q].astype(F32)
        pout[p, pl.ds(q * rowq, rowq)] = both.astype(BF)
        pass_on(q, 14, 14, p, ra2.at[q, 1], at(c, to, 0))

    total_stats = stat_s[...]
    for d in range(1, NBLK):
        pf = lax.rem(f - d + NBLK, NBLK)
        hid_copy(rstat.at[pf], rstat.at[pf], s3.at[pf], q3.at[pf], sg * NBLK + pf).wait_recv()
        total_stats = total_stats + rstat[pf]
    row_sq = jnp.sum(jnp.where(lane == experts, total_stats, 0.0), axis=1, keepdims=True)
    row_inverse = lax.rsqrt(row_sq * (1.0 / width) + 1e-05)
    logits = total_stats[:, 0:experts] * row_inverse + rb_ref[...]
    raised = jnp.where(mask > 0.5, jnp.exp(jnp.where(mask > 0.5, logits, 0.0)), 0.0)
    combine = (raised / jnp.sum(raised, axis=1, keepdims=True)).astype(BF)
    combine_wide = dot_nt(combine, expand_t)
    weights = jnp.where(chosen > 0.5, combine_wide, 0.0).astype(BF)

    for q in range(4):
        landed(q, 13, ra2.at[q, 0])
        landed(q, 14, ra2.at[q, 1])
        summed = tot[q * rowq : (q + 1) * rowq]
        summed = summed + ra2[q, 0].astype(F32) + ra2[q, 1].astype(F32)
        expert_out = summed + db_s[:, lanes(f)]
        zbout[q * quart : (q + 1) * quart] = expert_out.reshape(quart, SLOTS, BLK).astype(BF)

        @pl.loop(q * quart, (q + 1) * quart)
        def _(p):
            @pl.when(p != g)
            def _():
                req_copy(zbout.at[p], zbin.at[g], s6.at[p], q6.at[g], p).start()

    zbin[g] = zbout[g]

    @pl.loop(1, n_req)
    def _(d):
        p = lax.rem(g - d + n_req, n_req)
        req_copy(zbin.at[p], zbin.at[p], s6.at[p], q6.at[p], p).wait_recv()

    returned = zbin[...].astype(F32).reshape(pairs, BLK).astype(BF)
    mixture = jnp.dot(weights, returned, preferred_element_type=F32)
    first = jnp.where(sg == 0, 1.0, 0.0)
    fin_s[...] = (mixture + stream_wide * first).astype(BF)

    @pl.loop(1, n_hid)
    def _(d):
        p = lax.rem(h + d, n_hid)
        hid_copy(fin_s, rfin.at[h], s7.at[p], q7.at[h], p).start()

    rfin[h] = fin_s[...]

    @pl.loop(1, n_hid)
    def _(d):
        p = lax.rem(h - d + n_hid, n_hid)
        hid_copy(rfin.at[p], rfin.at[p], s7.at[p], q7.at[p], p).wait_recv()

    for b in range(NBLK):
        size = min(BLK, width - b * BLK)
        both = rfin[b].astype(F32) + rfin[NBLK + b].astype(F32)
        out_ref[:, b * BLK : b * BLK + size] = both[:, :size].astype(BF)

    for q in range(4):

        @pl.loop(0, 15)
        def _(k):
            hid_copy(piece(h, q), piece(h, q), s4.at[q, k], q4.at[h, q], at(0, 1, 0)).wait_send()
            hid_copy(part(h, q), part(h, q), s5.at[q, k], q5.at[q, k], at(0, 1, 0)).wait_send()

    @pl.loop(1, n_hid)
    def _(d):
        p = lax.rem(h + d, n_hid)
        hid_copy(r1.at[p], r1.at[p], s1.at[p], q1.at[p], p).wait_send()
        hid_copy(fin_s, rfin.at[p], s7.at[p], q7.at[p], p).wait_send()

    @pl.loop(1, NBLK)
    def _(d):
        pf = lax.rem(f + d, NBLK)
        hid_copy(stat_s, rstat.at[pf], s3.at[pf], q3.at[pf], sg * NBLK + pf).wait_send()

    @pl.loop(1, n_req)
    def _(d):
        p = lax.rem(g + d, n_req)
        req_copy(zout.at[p], ag.at[h, p], s2.at[p], q2.at[p], p).wait_send()
        req_copy(zbout.at[p], zbin.at[p], s6.at[p], q6.at[p], p).wait_send()


def on_device(
    attn_partial,
    residual,
    norm_gain,
    router_weight,
    router_bias,
    routes,
    gate_up,
    gate_up_bias,
    down_weight,
    down_bias,
):
    n_req, n_hid = lax.axis_size("req"), lax.axis_size("hid")
    rows, width = residual.shape
    wide = BLK * NBLK
    per = n_req * SLOTS
    vmem = pl.BlockSpec(memory_space=pltpu.VMEM)
    hbm = pl.BlockSpec(memory_space=pl.ANY)
    dma = pltpu.SemaphoreType.DMA
    hid_sem, req_sem = dma((n_hid,)), dma((n_req,))
    return pl.pallas_call(
        functools.partial(moe_kernel, n_req, n_hid),
        out_shape=jax.ShapeDtypeStruct((rows, width), BF),
        in_specs=[vmem] * 8 + [hbm] * 2,
        out_specs=vmem,
        scratch_shapes=[
            pltpu.VMEM((rows, wide), BF),
            pltpu.VMEM((rows, wide), BF),
            pltpu.VMEM((1, wide), F32),
            pltpu.VMEM((128, wide), BF),
            pltpu.VMEM((1, wide), F32),
            pltpu.VMEM(gate_up.shape[:0:-1], BF),
            pltpu.VMEM(down_weight.shape[1:], BF),
            pltpu.VMEM((512, wide), BF),
            pltpu.VMEM((256, wide), BF),
            pltpu.VMEM((n_hid, rows, BLK), BF),
            pltpu.VMEM((rows, 128), F32),
            pltpu.VMEM((NBLK, rows, 128), F32),
            pltpu.VMEM((n_req, SLOTS, BLK), BF),
            pltpu.VMEM((n_hid, n_req, SLOTS, BLK), BF),
            pltpu.VMEM((2, per, 512), F32),
            pltpu.VMEM((2, per, 128), F32),
            pltpu.VMEM((2, per, 256), BF),
            pltpu.VMEM((n_hid, per, BLK), BF),
            pltpu.VMEM((per, BLK), F32),
            pltpu.VMEM((4, 4, per // 4, BLK), BF),
            pltpu.VMEM((4, 4, 2, per // 4, BLK), BF),
            pltpu.VMEM((4, per // 4, BLK), BF),
            pltpu.VMEM((4, 2, per // 4, BLK), BF),
            pltpu.VMEM((n_req, SLOTS, BLK), BF),
            pltpu.VMEM((n_req, SLOTS, BLK), BF),
            pltpu.VMEM((rows, BLK), BF),
            pltpu.VMEM((n_hid, rows, BLK), BF),
            dma((2,)),
            hid_sem,
            hid_sem,
            req_sem,
            req_sem,
            dma((NBLK,)),
            dma((NBLK,)),
            dma((4, 15)),
            dma((n_hid, 4)),
            dma((4, 15)),
            dma((4, 15)),
            req_sem,
            req_sem,
            hid_sem,
            hid_sem,
        ],
        compiler_params=pltpu.CompilerParams(
            collective_id=0, has_side_effects=True, vmem_limit_bytes=56 * 1024 * 1024
        ),
        name="moe_block",
    )(
        attn_partial[0],
        residual,
        norm_gain.reshape(1, width),
        router_weight.T,
        router_bias.reshape(1, -1),
        routes.T,
        gate_up_bias,
        down_bias,
        gate_up[0].T,
        down_weight[0],
    )


def solution(mesh):
    return jax.shard_map(
        on_device,
        mesh=mesh,
        in_specs=(
            P("hid", "req", None),
            P("req", None),
            P(),
            P(),
            P(),
            P("req", None),
            P("req", None, "hid"),
            P("req", "hid"),
            P("req", "hid", None),
            P("req", None),
        ),
        out_specs=P("req", None),
        check_vma=False,
    )
```

```python
import functools

import jax
import jax.numpy as jnp
from jax import lax
from jax.experimental import pallas as pl
from jax.experimental.pallas import tpu as pltpu
from jax.sharding import PartitionSpec as P

MESH = pl.DeviceIdType.MESH
BLK = 384
NBLK = 8
SLOTS = 8
BF = jnp.bfloat16
F32 = jnp.float32


def lanes(block):
    return pl.ds(pl.multiple_of(block * BLK, 128), BLK)


def dot_nt(left, right):
    return lax.dot_general(
        left, right, (((1,), (1,)), ((), ())), preferred_element_type=F32
    )


def moe_kernel(
    n_req,
    n_hid,
    attn_ref,
    resid_ref,
    gain_ref,
    wr_ref,
    rb_ref,
    routes_ref,
    bgu_ref,
    db_ref,
    wgu_hbm,
    wd_hbm,
    out_ref,
    attn_s,
    resid_s,
    gain_s,
    wr_s,
    db_s,
    wgu_v,
    wd_v,
    wg_s,
    wd_s,
    mid1,
    sum1,
    rb1_1,
    rb2_1,
    ra1_1,
    ra2_1,
    stat_s,
    rstat,
    zout,
    ag,
    acc,
    ssq,
    act_s,
    pout,
    mid5,
    sum5,
    rb1,
    rb2,
    ra1,
    ra2,
    zbout,
    zbin,
    rfin,
    w_sem,
    s1,
    q1,
    s2,
    q2,
    s3,
    q3,
    s4,
    q4,
    s5,
    q5,
    s6,
    q6,
    s7,
    q7,
):
    rows, width = attn_ref.shape
    experts = rb_ref.shape[1]
    half = wd_hbm.shape[0]
    wide = BLK * NBLK
    tail = wide - 256
    h = lax.axis_index("hid")
    g = lax.axis_index("req")
    sg = lax.div(h, NBLK)
    f = lax.rem(h, NBLK)

    get_wgu = pltpu.make_async_copy(wgu_hbm, wgu_v, w_sem.at[0])
    get_wd = pltpu.make_async_copy(wd_hbm, wd_v, w_sem.at[1])
    get_wgu.start()
    get_wd.start()

    barrier = pltpu.get_barrier_semaphore()

    @pl.loop(1, n_hid)
    def _(d):
        pl.semaphore_signal(
            barrier, inc=1, device_id={"hid": lax.rem(h + d, n_hid)}, device_id_type=MESH
        )

    @pl.loop(1, n_req)
    def _(d):
        pl.semaphore_signal(
            barrier, inc=1, device_id={"req": lax.rem(g + d, n_req)}, device_id_type=MESH
        )

    attn_s[:, tail:] = jnp.zeros((rows, wide - tail), BF)
    attn_s[:, :width] = attn_ref[...]
    resid_s[:, tail:] = jnp.zeros((rows, wide - tail), BF)
    resid_s[:, :width] = resid_ref[...]
    gain_s[:, tail:] = jnp.zeros((1, wide - tail), F32)
    gain_s[:, :width] = gain_ref[...].reshape(1, width).astype(F32)
    db_s[:, tail:] = jnp.zeros((1, wide - tail), F32)
    db_s[:, :width] = db_ref[...].astype(F32)

    pl.semaphore_wait(barrier, n_hid + n_req - 2)

    def hid_copy(src, dst, send, recv, peer):
        return pltpu.make_async_remote_copy(
            src_ref=src,
            dst_ref=dst,
            send_sem=send,
            recv_sem=recv,
            device_id={"hid": peer},
            device_id_type=MESH,
        )

    def req_copy(src, dst, send, recv, peer):
        return pltpu.make_async_remote_copy(
            src_ref=src,
            dst_ref=dst,
            send_sem=send,
            recv_sem=recv,
            device_id={"req": peer},
            device_id_type=MESH,
        )

    side = 4
    x = lax.div(h, side)
    y = lax.rem(h, side)

    def at(c, da, db):
        a = lax.rem((x if c == 0 else y) + da, side)
        b = lax.rem((y if c == 0 else x) + db, side)
        return a * side + b if c == 0 else b * side + a

    def scatter_first(src, bufs, sems, make):
        rb1 = bufs[2]
        rb2 = bufs[3]

        def send(q, k, ref, dst, peer):
            hid_copy(ref, dst, sems[0].at[q, k], sems[1].at[q, k], peer).start()

        @pl.loop(0, 4)
        def _(j):
            for c in range(2):
                make(at(c, j, 2), c)
            for q in range(4):
                c, odd = q // 2, q % 2
                peer = at(c, 0, 1) if odd else at(c, 0, 3)
                send(q, j, src(at(c, j, 2), q), rb1.at[q, j], peer)

        @pl.loop(0, 4)
        def _(j):
            for c in range(2):
                make(at(c, j, 1), c)
                make(at(c, j, 3), c)
            for q in range(4):
                c, odd = q // 2, q % 2
                to = 3 if odd else 1
                send(q, 4 + j, src(at(c, j, to), q), rb2.at[q, j, 0], at(c, 0, to))

    def scatter_rest(src, bufs, sems, make):
        mid, sums, rb1, rb2, ra1, ra2 = bufs

        def send(q, k, ref, dst, peer):
            hid_copy(ref, dst, sems[0].at[q, k], sems[1].at[q, k], peer).start()

        def landed(q, k, dst):
            hid_copy(dst, dst, sems[0].at[q, 0], sems[1].at[q, k], at(0, 1, 0)).wait_recv()

        @pl.loop(0, 4)
        def _(j):
            for q in range(4):
                c, odd = q // 2, q % 2
                to = 1 if odd else 3
                landed(q, j, rb1.at[q, j])
                both = src(at(c, j, to), q)[...].astype(F32) + rb1[q, j].astype(F32)
                mid[q, j] = both.astype(BF)
                send(q, 8 + j, mid.at[q, j], rb2.at[q, j, 1], at(c, 0, to))
            for c in range(2):
                make(at(c, j, 0), c)

        def line_sum(j, q):
            landed(q, 4 + j, rb2.at[q, j, 0])
            landed(q, 8 + j, rb2.at[q, j, 1])
            three = src(at(q // 2, j, 0), q)[...].astype(F32)
            return three + rb2[q, j, 0].astype(F32) + rb2[q, j, 1].astype(F32)

        for q in range(4):
            c, odd = q // 2, q % 2
            sums[q, 2] = line_sum(2, q).astype(BF)
            send(q, 12, sums.at[q, 2], ra1.at[q], at(c, 1 if odd else 3, 0))
        for q in range(4):
            c, odd = q // 2, q % 2
            to = 3 if odd else 1
            sums[q, to] = line_sum(to, q).astype(BF)
            send(q, 13, sums.at[q, to], ra2.at[q, 0], at(c, to, 0))
        for q in range(4):
            c, odd = q // 2, q % 2
            to = 1 if odd else 3
            near = line_sum(to, q)
            landed(q, 12, ra1.at[q])
            sums[q, to] = (near + ra1[q].astype(F32)).astype(BF)
            send(q, 14, sums.at[q, to], ra2.at[q, 1], at(c, to, 0))

        def result(q):
            total = line_sum(0, q)
            landed(q, 13, ra2.at[q, 0])
            landed(q, 14, ra2.at[q, 1])
            return total + ra2[q, 0].astype(F32) + ra2[q, 1].astype(F32)

        return result

    def gather_over_hid(piece, sems, ready, after):
        def ship(q, k, p, peer):
            ref = piece(p, q)
            hid_copy(ref, ref, sems[0].at[q, k], sems[1].at[p, q], peer).start()

        def arrive(q, p):
            ref = piece(p, q)
            hid_copy(ref, ref, sems[0].at[q, 0], sems[1].at[p, q], p).wait_recv()

        for q in range(4):
            c = q // 2
            ready(q)
            ship(q, 0, h, at(c, 1, 0))
            ship(q, 1, h, at(c, 3, 0))
            ship(q, 3, h, at(c, 0, 1))
            ship(q, 4, h, at(c, 0, 3))
        for c in range(2):
            after(h, c)
        for q in range(4):
            c, odd = q // 2, q % 2
            arrive(q, at(c, 1, 0))
            arrive(q, at(c, 3, 0))
            if odd:
                ship(q, 2, at(c, 1, 0), at(c, 3, 0))
            else:
                ship(q, 2, at(c, 3, 0), at(c, 1, 0))
            for j in (1, 3):
                ship(q, 3 + 2 * j, at(c, j, 0), at(c, 0, 1))
                ship(q, 4 + 2 * j, at(c, j, 0), at(c, 0, 3))
        for c in range(2):

            @pl.loop(0, 2)
            def _(i):
                after(at(c, 2 * i + 1, 0), c)

        for q in range(4):
            c = q // 2
            arrive(q, at(c, 2, 0))
            ship(q, 7, at(c, 2, 0), at(c, 0, 1))
            ship(q, 8, at(c, 2, 0), at(c, 0, 3))

        @pl.loop(0, 4)
        def _(i):
            j = lax.rem(i + i + i, 4)
            for q in range(4):
                c, odd = q // 2, q % 2
                arrive(q, at(c, j, 1))
                arrive(q, at(c, j, 3))
                if odd:
                    ship(q, 11 + j, at(c, j, 1), at(c, 0, 3))
                else:
                    ship(q, 11 + j, at(c, j, 3), at(c, 0, 1))

        for c in range(2):
            after(at(c, 2, 0), c)

            @pl.loop(0, 4)
            def _(j):
                after(at(c, j, 1), c)
                after(at(c, j, 3), c)

        @pl.loop(0, 4)
        def _(i):
            j = lax.rem(i + i + i, 4)
            for q in range(4):
                arrive(q, at(q // 2, j, 2))
            for c in range(2):
                after(at(c, j, 2), c)

    def sent(refs, sems):
        for q in range(4):

            @pl.loop(0, 15)
            def _(k):
                ref = refs(q)
                hid_copy(ref, ref, sems[0].at[q, k], sems[0].at[q, k], at(0, 1, 0)).wait_send()

    def nothing(p, c):
        pass

    bufs1 = (mid1, sum1, rb1_1, rb2_1, ra1_1, ra2_1)
    rowq1 = rows // 4

    def share(p, q):
        return attn_s.at[pl.ds(q * rowq1, rowq1), lanes(lax.rem(p, NBLK))]

    scatter_first(share, bufs1, (s1, q1), nothing)

    wr_s[...] = jnp.zeros(wr_s.shape, BF)
    wr_s[0:experts, 0:width] = wr_ref[...]
    named = lax.broadcasted_iota(jnp.int32, (experts, rows), 0)
    mask_t = jnp.zeros((experts, rows), F32)
    for k in range(routes_ref.shape[0]):
        mask_t = mask_t + jnp.where(routes_ref[k : k + 1, :] == named, 1.0, 0.0)
    row_a = lax.broadcasted_iota(jnp.int32, (rows, rows), 0)
    row_b = lax.broadcasted_iota(jnp.int32, (rows, rows), 1)
    same = (row_a == row_b).astype(BF)
    mask_t = mask_t.astype(BF)
    slot_t = jnp.dot(mask_t, (row_a < row_b).astype(BF), preferred_element_type=F32)
    pairs = experts * SLOTS
    col = lax.broadcasted_iota(jnp.int32, (pairs, experts), 0)
    own = lax.broadcasted_iota(jnp.int32, (pairs, experts), 1)
    expand_t = (lax.div(col, SLOTS) == own).astype(BF)
    slot_wide = jnp.dot(expand_t, slot_t.astype(BF), preferred_element_type=F32)
    mask_wide = jnp.dot(expand_t, mask_t, preferred_element_type=F32)
    want = lax.rem(lax.broadcasted_iota(jnp.int32, (pairs, rows), 0), SLOTS) + sg * SLOTS
    chosen_t = jnp.where((slot_wide == want.astype(F32)) & (mask_wide > 0.5), 1.0, 0.0)
    chosen_t = chosen_t.astype(BF)
    chosen = dot_nt(same, chosen_t)
    mask = dot_nt(same, mask_t)

    result1 = scatter_rest(share, bufs1, (s1, q1), nothing)
    attention = jnp.concatenate([result1(q) for q in range(4)], axis=0)
    stream = (resid_s[:, lanes(f)].astype(F32) + attention).astype(BF)
    stream_wide = stream.astype(F32)

    picked = jnp.dot(chosen_t, stream, preferred_element_type=F32)
    zout[...] = picked.reshape(experts, SLOTS, BLK).astype(BF)

    @pl.loop(1, n_req)
    def _(i):
        step = lax.div(i + 1, 2)
        d = step + lax.rem(i + 1, 2) * (n_req - 2 * step)
        p = lax.rem(g + d, n_req)
        req_copy(zout.at[p], ag.at[h, g], s2.at[p], q2.at[g], p).start()

    scaled = (stream_wide * gain_s[:, lanes(f)]).astype(BF)
    stats = dot_nt(scaled, wr_s[:, lanes(f)])
    squares = jnp.sum(stream_wide * stream_wide, axis=1, keepdims=True)
    lane = lax.broadcasted_iota(jnp.int32, (rows, 128), 1)
    stat_s[...] = jnp.where(lane == experts, squares, stats)

    @pl.loop(1, NBLK)
    def _(d):
        pf = lax.rem(f + d, NBLK)
        hid_copy(
            stat_s, rstat.at[f], s3.at[pf], q3.at[f], sg * NBLK + pf
        ).start()

    get_wgu.wait()
    twice = wgu_v.shape[0]
    from_col = lax.broadcasted_iota(jnp.int32, (512, twice), 1)
    to_col = lax.broadcasted_iota(jnp.int32, (512, twice), 0)
    perm = (to_col == lax.rem(from_col, 2) * 256 + lax.div(from_col, 2)).astype(BF)
    wg_s[:, tail:] = jnp.zeros((512, wide - tail), BF)

    @pl.loop(0, width // BLK)
    def _(i):
        at = lanes(i)
        wg_s[:, at] = jnp.dot(perm, wgu_v[:, at], preferred_element_type=F32).astype(BF)

    last = width // BLK * BLK
    wg_s[:, last:width] = jnp.dot(
        perm, wgu_v[:, last:width], preferred_element_type=F32
    ).astype(BF)
    bias = dot_nt(jnp.broadcast_to(bgu_ref[...], (16, twice)), perm)[0:1, :]
    get_wd.wait()
    wd_s[...] = jnp.zeros(wd_s.shape, BF)
    wd_s[0:half, 0:width] = wd_v[...]
    acc[...] = jnp.zeros(acc.shape, F32)
    ssq[...] = jnp.zeros(ssq.shape, F32)

    quart = n_req // 4
    half0 = lax.div(g, 2 * quart)

    def group_at(q):
        return lax.rem(half0 + q // 2, 2) * (2 * quart) + q % 2 * quart

    def piece(p, q):
        return ag.at[p, pl.ds(group_at(q), quart)]

    def use_half(p, c):
        first = group_at(2 * c)
        wide_rows = ag[p, pl.ds(first, 2 * quart)].astype(F32)
        count = 2 * quart * SLOTS
        wide_rows = wide_rows.reshape(count, BLK)
        to = lax.div(p, NBLK)
        blk = lax.rem(p, NBLK)
        sq = wide_rows * wide_rows
        here = pl.ds(pl.multiple_of(first * SLOTS, count), count)
        ssq[to, here] += sq[:, 0:128] + sq[:, 128:256] + sq[:, 256:384]
        u = (wide_rows * gain_s[:, lanes(blk)]).astype(BF)
        acc[to, here] += dot_nt(u, wg_s[:, lanes(blk)])

    def arrived(q):
        @pl.loop(0, quart)
        def _(i):
            p = group_at(q) + i

            @pl.when(p != g)
            def _():
                req_copy(zout.at[p], ag.at[h, p], s2.at[p], q2.at[p], p).wait_recv()

    ag[h, g] = zout[g]
    gather_over_hid(piece, (s4, q4), arrived, use_half)

    for side_at in range(2):
        mean = jnp.sum(ssq[side_at], axis=1, keepdims=True) * (1.0 / width)
        inverse = lax.rsqrt(mean + 1e-05)
        gate = jnp.minimum(acc[side_at, :, 0:256] * inverse + bias[:, 0:256], 7.0)
        up = jnp.clip(acc[side_at, :, 256:512] * inverse + bias[:, 256:512], -7.0, 7.0)
        act_s[side_at] = ((up + 1.0) * gate * jax.nn.sigmoid(1.702 * gate)).astype(BF)

    rowq = quart * SLOTS

    def down(p, c):
        here = slice(c * 2 * rowq, (c + 1) * 2 * rowq)
        pout[p, here] = jnp.dot(
            act_s[lax.div(p, NBLK), here],
            wd_s[:, lanes(lax.rem(p, NBLK))],
            preferred_element_type=F32,
        ).astype(BF)

    def part(p, q):
        return pout.at[p, pl.ds(q * rowq, rowq)]

    bufs5 = (mid5, sum5, rb1, rb2, ra1, ra2)
    scatter_first(part, bufs5, (s5, q5), down)
    result5 = scatter_rest(part, bufs5, (s5, q5), down)

    total_stats = stat_s[...]
    for d in range(1, NBLK):
        pf = lax.rem(f - d + NBLK, NBLK)
        hid_copy(rstat.at[pf], rstat.at[pf], s3.at[pf], q3.at[pf], sg * NBLK + pf).wait_recv()
        total_stats = total_stats + rstat[pf]
    row_sq = jnp.sum(jnp.where(lane == experts, total_stats, 0.0), axis=1, keepdims=True)
    row_inverse = lax.rsqrt(row_sq * (1.0 / width) + 1e-05)
    logits = total_stats[:, 0:experts] * row_inverse + rb_ref[...]
    raised = jnp.where(mask > 0.5, jnp.exp(jnp.where(mask > 0.5, logits, 0.0)), 0.0)
    combine = (raised / jnp.sum(raised, axis=1, keepdims=True)).astype(BF)
    combine_wide = dot_nt(combine, expand_t)
    weights = jnp.where(chosen > 0.5, combine_wide, 0.0).astype(BF)

    for q in range(4):
        expert_out = result5(q) + db_s[:, lanes(f)]
        zbout[q * quart : (q + 1) * quart] = expert_out.reshape(quart, SLOTS, BLK).astype(BF)

        @pl.loop(q * quart, (q + 1) * quart)
        def _(p):
            @pl.when(p != g)
            def _():
                req_copy(zbout.at[p], zbin.at[g], s6.at[p], q6.at[g], p).start()

    zbin[g] = zbout[g]

    @pl.loop(1, n_req)
    def _(d):
        p = lax.rem(g - d + n_req, n_req)
        req_copy(zbin.at[p], zbin.at[p], s6.at[p], q6.at[p], p).wait_recv()

    returned = zbin[...].astype(F32).reshape(pairs, BLK).astype(BF)
    mixture = jnp.dot(weights, returned, preferred_element_type=F32)
    first = jnp.where(sg == 0, 1.0, 0.0)
    rfin[h] = (mixture + stream_wide * first).astype(BF)

    def final(p, q):
        return rfin.at[p, pl.ds(q * rowq1, rowq1)]

    gather_over_hid(final, (s7, q7), lambda q: None, nothing)

    for b in range(NBLK):
        size = min(BLK, width - b * BLK)
        both = rfin[b].astype(F32) + rfin[NBLK + b].astype(F32)
        out_ref[:, b * BLK : b * BLK + size] = both[:, :size].astype(BF)

    sent(lambda q: share(h, q), (s1, q1))
    sent(lambda q: piece(h, q), (s4, q4))
    sent(lambda q: part(h, q), (s5, q5))
    sent(lambda q: final(h, q), (s7, q7))

    @pl.loop(1, NBLK)
    def _(d):
        pf = lax.rem(f + d, NBLK)
        hid_copy(stat_s, rstat.at[pf], s3.at[pf], q3.at[pf], sg * NBLK + pf).wait_send()

    @pl.loop(1, n_req)
    def _(d):
        p = lax.rem(g + d, n_req)
        req_copy(zout.at[p], ag.at[h, p], s2.at[p], q2.at[p], p).wait_send()
        req_copy(zbout.at[p], zbin.at[p], s6.at[p], q6.at[p], p).wait_send()


def ring_buffers(size):
    return [
        pltpu.VMEM((4, 4, size, BLK), BF),
        pltpu.VMEM((4, 4, size, BLK), BF),
        pltpu.VMEM((4, 4, size, BLK), BF),
        pltpu.VMEM((4, 4, 2, size, BLK), BF),
        pltpu.VMEM((4, size, BLK), BF),
        pltpu.VMEM((4, 2, size, BLK), BF),
    ]


def on_device(
    attn_partial,
    residual,
    norm_gain,
    router_weight,
    router_bias,
    routes,
    gate_up,
    gate_up_bias,
    down_weight,
    down_bias,
):
    n_req, n_hid = lax.axis_size("req"), lax.axis_size("hid")
    rows, width = residual.shape
    wide = BLK * NBLK
    per = n_req * SLOTS
    vmem = pl.BlockSpec(memory_space=pltpu.VMEM)
    hbm = pl.BlockSpec(memory_space=pl.ANY)
    dma = pltpu.SemaphoreType.DMA
    hid_sem, req_sem = dma((n_hid,)), dma((n_req,))
    return pl.pallas_call(
        functools.partial(moe_kernel, n_req, n_hid),
        out_shape=jax.ShapeDtypeStruct((rows, width), BF),
        in_specs=[vmem] * 8 + [hbm] * 2,
        out_specs=vmem,
        scratch_shapes=[
            pltpu.VMEM((rows, wide), BF),
            pltpu.VMEM((rows, wide), BF),
            pltpu.VMEM((1, wide), F32),
            pltpu.VMEM((128, wide), BF),
            pltpu.VMEM((1, wide), F32),
            pltpu.VMEM(gate_up.shape[:0:-1], BF),
            pltpu.VMEM(down_weight.shape[1:], BF),
            pltpu.VMEM((512, wide), BF),
            pltpu.VMEM((256, wide), BF),
            *ring_buffers(rows // 4),
            pltpu.VMEM((rows, 128), F32),
            pltpu.VMEM((NBLK, rows, 128), F32),
            pltpu.VMEM((n_req, SLOTS, BLK), BF),
            pltpu.VMEM((n_hid, n_req, SLOTS, BLK), BF),
            pltpu.VMEM((2, per, 512), F32),
            pltpu.VMEM((2, per, 128), F32),
            pltpu.VMEM((2, per, 256), BF),
            pltpu.VMEM((n_hid, per, BLK), BF),
            *ring_buffers(per // 4),
            pltpu.VMEM((n_req, SLOTS, BLK), BF),
            pltpu.VMEM((n_req, SLOTS, BLK), BF),
            pltpu.VMEM((n_hid, rows, BLK), BF),
            dma((2,)),
            dma((4, 15)),
            dma((4, 15)),
            req_sem,
            req_sem,
            dma((NBLK,)),
            dma((NBLK,)),
            dma((4, 15)),
            dma((n_hid, 4)),
            dma((4, 15)),
            dma((4, 15)),
            req_sem,
            req_sem,
            dma((4, 15)),
            dma((n_hid, 4)),
        ],
        compiler_params=pltpu.CompilerParams(
            collective_id=0, has_side_effects=True, vmem_limit_bytes=56 * 1024 * 1024
        ),
        name="moe_block",
    )(
        attn_partial[0],
        residual,
        norm_gain,
        router_weight.T,
        router_bias.reshape(1, -1),
        routes.T,
        gate_up_bias,
        down_bias,
        gate_up[0].T,
        down_weight[0],
    )


def solution(mesh):
    return jax.shard_map(
        on_device,
        mesh=mesh,
        in_specs=(
            P("hid", "req", None),
            P("req", None),
            P(),
            P(),
            P(),
            P("req", None),
            P("req", None, "hid"),
            P("req", "hid"),
            P("req", "hid", None),
            P("req", None),
        ),
        out_specs=P("req", None),
        check_vma=False,
    )
```

```python
import functools

import jax
import jax.numpy as jnp
from jax import lax
from jax.experimental import pallas as pl
from jax.experimental.pallas import tpu as pltpu
from jax.sharding import PartitionSpec as P

MESH = pl.DeviceIdType.MESH
BLK = 384
NBLK = 8
SLOTS = 8
BF = jnp.bfloat16
F32 = jnp.float32


def lanes(block):
    return pl.ds(pl.multiple_of(block * BLK, 128), BLK)


def dot_nt(left, right):
    return lax.dot_general(
        left, right, (((1,), (1,)), ((), ())), preferred_element_type=F32
    )


def moe_kernel(
    n_req,
    n_hid,
    attn_hbm,
    resid_hbm,
    gain_ref,
    wr_ref,
    rb_ref,
    routes_ref,
    bgu_ref,
    db_ref,
    wgu_hbm,
    wd_hbm,
    out_ref,
    attn_v,
    resid_v,
    attn_s,
    resid_s,
    gain_s,
    wr_s,
    db_s,
    wgu_v,
    wd_v,
    wg_s,
    wd_s,
    mid1,
    sum1,
    rb1_1,
    rb2_1,
    ra1_1,
    ra2_1,
    stat_s,
    rstat,
    zout,
    ag,
    acc,
    ssq,
    act_s,
    pout,
    mid5,
    sum5,
    rb1,
    rb2,
    ra1,
    ra2,
    zbout,
    zbin,
    rfin,
    w_sem,
    s1,
    q1,
    s2,
    q2,
    s3,
    q3,
    s4,
    q4,
    s5,
    q5,
    s6,
    q6,
    s7,
    q7,
):
    rows, width = attn_hbm.shape
    experts = rb_ref.shape[1]
    half = wd_hbm.shape[0]
    wide = BLK * NBLK
    tail = wide - 256
    h = lax.axis_index("hid")
    g = lax.axis_index("req")
    sg = lax.div(h, NBLK)
    f = lax.rem(h, NBLK)

    get_attn = pltpu.make_async_copy(attn_hbm, attn_v, w_sem.at[2])
    get_resid = pltpu.make_async_copy(resid_hbm, resid_v, w_sem.at[3])
    get_attn.start()
    get_resid.start()
    get_wgu = pltpu.make_async_copy(wgu_hbm, wgu_v, w_sem.at[0])
    get_wd = pltpu.make_async_copy(wd_hbm, wd_v, w_sem.at[1])
    get_wgu.start()
    get_wd.start()

    barrier = pltpu.get_barrier_semaphore()

    @pl.loop(1, n_req)
    def _(i):
        step = lax.div(n_req + 1 - i, 2)
        d = step + lax.rem(n_req + 1 - i, 2) * (n_req - 2 * step)
        pl.semaphore_signal(
            barrier, inc=1, device_id={"req": lax.rem(g + d, n_req)}, device_id_type=MESH
        )

    @pl.loop(1, n_hid)
    def _(d):
        pl.semaphore_signal(
            barrier, inc=1, device_id={"hid": lax.rem(h + d, n_hid)}, device_id_type=MESH
        )

    attn_s[:, tail:] = jnp.zeros((rows, wide - tail), BF)
    get_attn.wait()
    attn_s[:, :width] = attn_v[...]
    resid_s[:, tail:] = jnp.zeros((rows, wide - tail), BF)
    get_resid.wait()
    resid_s[:, :width] = resid_v[...]
    gain_s[:, tail:] = jnp.zeros((1, wide - tail), F32)
    gain_s[:, :width] = gain_ref[...].reshape(1, width).astype(F32)
    db_s[:, tail:] = jnp.zeros((1, wide - tail), F32)
    db_s[:, :width] = db_ref[...].astype(F32)

    pl.semaphore_wait(barrier, n_hid + n_req - 2)

    def hid_copy(src, dst, send, recv, peer):
        return pltpu.make_async_remote_copy(
            src_ref=src,
            dst_ref=dst,
            send_sem=send,
            recv_sem=recv,
            device_id={"hid": peer},
            device_id_type=MESH,
        )

    def req_copy(src, dst, send, recv, peer):
        return pltpu.make_async_remote_copy(
            src_ref=src,
            dst_ref=dst,
            send_sem=send,
            recv_sem=recv,
            device_id={"req": peer},
            device_id_type=MESH,
        )

    side = 4
    x = lax.div(h, side)
    y = lax.rem(h, side)

    def at(c, da, db):
        a = lax.rem((x if c == 0 else y) + da, side)
        b = lax.rem((y if c == 0 else x) + db, side)
        return a * side + b if c == 0 else b * side + a

    def scatter_first(src, bufs, sems, make):
        rb1 = bufs[2]
        rb2 = bufs[3]

        def send(q, k, ref, dst, peer):
            hid_copy(ref, dst, sems[0].at[q, k], sems[1].at[q, k], peer).start()

        @pl.loop(0, 4)
        def _(j):
            for c in range(2):
                make(at(c, j, 2), c)
            for q in range(4):
                c, odd = q // 2, q % 2
                peer = at(c, 0, 1) if odd else at(c, 0, 3)
                send(q, j, src(at(c, j, 2), q), rb1.at[q, j], peer)

        @pl.loop(0, 4)
        def _(j):
            for c in range(2):
                make(at(c, j, 1), c)
                make(at(c, j, 3), c)
            for q in range(4):
                c, odd = q // 2, q % 2
                to = 3 if odd else 1
                send(q, 4 + j, src(at(c, j, to), q), rb2.at[q, j, 0], at(c, 0, to))

    def scatter_rest(src, bufs, sems, make):
        mid, sums, rb1, rb2, ra1, ra2 = bufs

        def send(q, k, ref, dst, peer):
            hid_copy(ref, dst, sems[0].at[q, k], sems[1].at[q, k], peer).start()

        def landed(q, k, dst):
            hid_copy(dst, dst, sems[0].at[q, 0], sems[1].at[q, k], at(0, 1, 0)).wait_recv()

        @pl.loop(0, 4)
        def _(j):
            for q in range(4):
                c, odd = q // 2, q % 2
                to = 1 if odd else 3
                landed(q, j, rb1.at[q, j])
                both = src(at(c, j, to), q)[...].astype(F32) + rb1[q, j].astype(F32)
                mid[q, j] = both.astype(BF)
                send(q, 8 + j, mid.at[q, j], rb2.at[q, j, 1], at(c, 0, to))
            for c in range(2):
                make(at(c, j, 0), c)

        def line_sum(j, q):
            landed(q, 4 + j, rb2.at[q, j, 0])
            landed(q, 8 + j, rb2.at[q, j, 1])
            three = src(at(q // 2, j, 0), q)[...].astype(F32)
            return three + rb2[q, j, 0].astype(F32) + rb2[q, j, 1].astype(F32)

        for q in range(4):
            c, odd = q // 2, q % 2
            sums[q, 2] = line_sum(2, q).astype(BF)
            send(q, 12, sums.at[q, 2], ra1.at[q], at(c, 1 if odd else 3, 0))
        for q in range(4):
            c, odd = q // 2, q % 2
            to = 3 if odd else 1
            sums[q, to] = line_sum(to, q).astype(BF)
            send(q, 13, sums.at[q, to], ra2.at[q, 0], at(c, to, 0))
        for q in range(4):
            c, odd = q // 2, q % 2
            to = 1 if odd else 3
            near = line_sum(to, q)
            landed(q, 12, ra1.at[q])
            sums[q, to] = (near + ra1[q].astype(F32)).astype(BF)
            send(q, 14, sums.at[q, to], ra2.at[q, 1], at(c, to, 0))

        def result(q):
            total = line_sum(0, q)
            landed(q, 13, ra2.at[q, 0])
            landed(q, 14, ra2.at[q, 1])
            return total + ra2[q, 0].astype(F32) + ra2[q, 1].astype(F32)

        return result

    def gather_over_hid(piece, sems, ready, after):
        def ship(q, k, p, peer):
            ref = piece(p, q)
            hid_copy(ref, ref, sems[0].at[q, k], sems[1].at[p, q], peer).start()

        def arrive(q, p):
            ref = piece(p, q)
            hid_copy(ref, ref, sems[0].at[q, 0], sems[1].at[p, q], p).wait_recv()

        for q in range(4):
            c = q // 2
            ready(q)
            ship(q, 0, h, at(c, 1, 0))
            ship(q, 1, h, at(c, 3, 0))
            ship(q, 3, h, at(c, 0, 1))
            ship(q, 4, h, at(c, 0, 3))
        for c in range(2):
            after(h, c)
        for q in range(4):
            c, odd = q // 2, q % 2
            arrive(q, at(c, 1, 0))
            arrive(q, at(c, 3, 0))
            if odd:
                ship(q, 2, at(c, 1, 0), at(c, 3, 0))
            else:
                ship(q, 2, at(c, 3, 0), at(c, 1, 0))
            for j in (1, 3):
                ship(q, 3 + 2 * j, at(c, j, 0), at(c, 0, 1))
                ship(q, 4 + 2 * j, at(c, j, 0), at(c, 0, 3))
        for c in range(2):

            @pl.loop(0, 2)
            def _(i):
                after(at(c, 2 * i + 1, 0), c)

        for q in range(4):
            c = q // 2
            arrive(q, at(c, 2, 0))
            ship(q, 7, at(c, 2, 0), at(c, 0, 1))
            ship(q, 8, at(c, 2, 0), at(c, 0, 3))

        @pl.loop(0, 4)
        def _(i):
            j = lax.rem(i + i + i, 4)
            for q in range(4):
                c, odd = q // 2, q % 2
                arrive(q, at(c, j, 1))
                arrive(q, at(c, j, 3))
                if odd:
                    ship(q, 11 + j, at(c, j, 1), at(c, 0, 3))
                else:
                    ship(q, 11 + j, at(c, j, 3), at(c, 0, 1))

        for c in range(2):
            after(at(c, 2, 0), c)

            @pl.loop(0, 4)
            def _(j):
                after(at(c, j, 1), c)
                after(at(c, j, 3), c)

        @pl.loop(0, 4)
        def _(i):
            j = lax.rem(i + i + i, 4)
            for q in range(4):
                arrive(q, at(q // 2, j, 2))
            for c in range(2):
                after(at(c, j, 2), c)

    def sent(refs, sems):
        for q in range(4):

            @pl.loop(0, 15)
            def _(k):
                ref = refs(q)
                hid_copy(ref, ref, sems[0].at[q, k], sems[0].at[q, k], at(0, 1, 0)).wait_send()

    def nothing(p, c):
        pass

    bufs1 = (mid1, sum1, rb1_1, rb2_1, ra1_1, ra2_1)
    rowq1 = rows // 4

    def share(p, q):
        return attn_s.at[pl.ds(q * rowq1, rowq1), lanes(lax.rem(p, NBLK))]

    scatter_first(share, bufs1, (s1, q1), nothing)

    wr_s[...] = jnp.zeros(wr_s.shape, BF)
    wr_s[0:experts, 0:width] = wr_ref[...]
    named = lax.broadcasted_iota(jnp.int32, (experts, rows), 0)
    mask_t = jnp.zeros((experts, rows), F32)
    for k in range(routes_ref.shape[0]):
        mask_t = mask_t + jnp.where(routes_ref[k : k + 1, :] == named, 1.0, 0.0)
    row_a = lax.broadcasted_iota(jnp.int32, (rows, rows), 0)
    row_b = lax.broadcasted_iota(jnp.int32, (rows, rows), 1)
    same = (row_a == row_b).astype(BF)
    mask_t = mask_t.astype(BF)
    slot_t = jnp.dot(mask_t, (row_a < row_b).astype(BF), preferred_element_type=F32)
    pairs = experts * SLOTS
    col = lax.broadcasted_iota(jnp.int32, (pairs, experts), 0)
    own = lax.broadcasted_iota(jnp.int32, (pairs, experts), 1)
    expand_t = (lax.div(col, SLOTS) == own).astype(BF)
    slot_wide = jnp.dot(expand_t, slot_t.astype(BF), preferred_element_type=F32)
    mask_wide = jnp.dot(expand_t, mask_t, preferred_element_type=F32)
    want = lax.rem(lax.broadcasted_iota(jnp.int32, (pairs, rows), 0), SLOTS) + sg * SLOTS
    chosen_t = jnp.where((slot_wide == want.astype(F32)) & (mask_wide > 0.5), 1.0, 0.0)
    chosen_t = chosen_t.astype(BF)
    chosen = dot_nt(same, chosen_t)
    mask = dot_nt(same, mask_t)

    result1 = scatter_rest(share, bufs1, (s1, q1), nothing)
    attention = jnp.concatenate([result1(q) for q in range(4)], axis=0)
    stream = (resid_s[:, lanes(f)].astype(F32) + attention).astype(BF)
    stream_wide = stream.astype(F32)

    picked = jnp.dot(chosen_t, stream, preferred_element_type=F32)
    zout[...] = picked.reshape(experts, SLOTS, BLK).astype(BF)

    @pl.loop(1, n_req)
    def _(i):
        step = lax.div(i + 1, 2)
        d = step + lax.rem(i + 1, 2) * (n_req - 2 * step)
        p = lax.rem(g + d, n_req)
        req_copy(zout.at[p], ag.at[h, g], s2.at[p], q2.at[g], p).start()

    scaled = (stream_wide * gain_s[:, lanes(f)]).astype(BF)
    stats = dot_nt(scaled, wr_s[:, lanes(f)])
    squares = jnp.sum(stream_wide * stream_wide, axis=1, keepdims=True)
    lane = lax.broadcasted_iota(jnp.int32, (rows, 128), 1)
    stat_s[...] = jnp.where(lane == experts, squares, stats)

    @pl.loop(1, NBLK)
    def _(d):
        pf = lax.rem(f + d, NBLK)
        hid_copy(
            stat_s, rstat.at[f], s3.at[pf], q3.at[f], sg * NBLK + pf
        ).start()

    get_wgu.wait()
    twice = wgu_v.shape[0]
    from_col = lax.broadcasted_iota(jnp.int32, (512, twice), 1)
    to_col = lax.broadcasted_iota(jnp.int32, (512, twice), 0)
    perm = (to_col == lax.rem(from_col, 2) * 256 + lax.div(from_col, 2)).astype(BF)
    wg_s[:, tail:] = jnp.zeros((512, wide - tail), BF)

    @pl.loop(0, width // BLK)
    def _(i):
        at = lanes(i)
        wg_s[:, at] = jnp.dot(perm, wgu_v[:, at], preferred_element_type=F32).astype(BF)

    last = width // BLK * BLK
    wg_s[:, last:width] = jnp.dot(
        perm, wgu_v[:, last:width], preferred_element_type=F32
    ).astype(BF)
    bias = dot_nt(jnp.broadcast_to(bgu_ref[...], (16, twice)), perm)[0:1, :]
    get_wd.wait()
    wd_s[...] = jnp.zeros(wd_s.shape, BF)
    wd_s[0:half, 0:width] = wd_v[...]
    acc[...] = jnp.zeros(acc.shape, F32)
    ssq[...] = jnp.zeros(ssq.shape, F32)

    quart = n_req // 4
    half0 = lax.div(g, 2 * quart)

    def group_at(q):
        return lax.rem(half0 + q // 2, 2) * (2 * quart) + q % 2 * quart

    def piece(p, q):
        return ag.at[p, pl.ds(group_at(q), quart)]

    def use_half(p, c):
        first = group_at(2 * c)
        wide_rows = ag[p, pl.ds(first, 2 * quart)].astype(F32)
        count = 2 * quart * SLOTS
        wide_rows = wide_rows.reshape(count, BLK)
        to = lax.div(p, NBLK)
        blk = lax.rem(p, NBLK)
        sq = wide_rows * wide_rows
        here = pl.ds(pl.multiple_of(first * SLOTS, count), count)
        ssq[to, here] += sq[:, 0:128] + sq[:, 128:256] + sq[:, 256:384]
        u = (wide_rows * gain_s[:, lanes(blk)]).astype(BF)
        acc[to, here] += dot_nt(u, wg_s[:, lanes(blk)])

    def arrived(q):
        @pl.loop(0, quart)
        def _(i):
            p = group_at(q) + i

            @pl.when(p != g)
            def _():
                req_copy(zout.at[p], ag.at[h, p], s2.at[p], q2.at[p], p).wait_recv()

    sent(lambda q: share(h, q), (s1, q1))
    ag[h, g] = zout[g]
    gather_over_hid(piece, (s4, q4), arrived, use_half)

    for side_at in range(2):
        mean = jnp.sum(ssq[side_at], axis=1, keepdims=True) * (1.0 / width)
        inverse = lax.rsqrt(mean + 1e-05)
        gate = jnp.minimum(acc[side_at, :, 0:256] * inverse + bias[:, 0:256], 7.0)
        up = jnp.clip(acc[side_at, :, 256:512] * inverse + bias[:, 256:512], -7.0, 7.0)
        act_s[side_at] = ((up + 1.0) * gate * jax.nn.sigmoid(1.702 * gate)).astype(BF)

    rowq = quart * SLOTS

    def down(p, c):
        here = slice(c * 2 * rowq, (c + 1) * 2 * rowq)
        pout[p, here] = jnp.dot(
            act_s[lax.div(p, NBLK), here],
            wd_s[:, lanes(lax.rem(p, NBLK))],
            preferred_element_type=F32,
        ).astype(BF)

    def part(p, q):
        return pout.at[p, pl.ds(q * rowq, rowq)]

    bufs5 = (mid5, sum5, rb1, rb2, ra1, ra2)
    scatter_first(part, bufs5, (s5, q5), down)
    total_stats = stat_s[...]
    for d in range(1, NBLK):
        pf = lax.rem(f - d + NBLK, NBLK)
        hid_copy(rstat.at[pf], rstat.at[pf], s3.at[pf], q3.at[pf], sg * NBLK + pf).wait_recv()
        total_stats = total_stats + rstat[pf]
    row_sq = jnp.sum(jnp.where(lane == experts, total_stats, 0.0), axis=1, keepdims=True)
    row_inverse = lax.rsqrt(row_sq * (1.0 / width) + 1e-05)
    logits = total_stats[:, 0:experts] * row_inverse + rb_ref[...]
    raised = jnp.where(mask > 0.5, jnp.exp(jnp.where(mask > 0.5, logits, 0.0)), 0.0)
    combine = (raised / jnp.sum(raised, axis=1, keepdims=True)).astype(BF)
    combine_wide = dot_nt(combine, expand_t)
    weights = jnp.where(chosen > 0.5, combine_wide, 0.0).astype(BF)

    result5 = scatter_rest(part, bufs5, (s5, q5), down)

    for q in range(4):
        expert_out = result5(q) + db_s[:, lanes(f)]
        zbout[q * quart : (q + 1) * quart] = expert_out.reshape(quart, SLOTS, BLK).astype(BF)

        @pl.loop(q * quart, (q + 1) * quart)
        def _(p):
            @pl.when(p != g)
            def _():
                req_copy(zbout.at[p], zbin.at[g], s6.at[p], q6.at[g], p).start()

    zbin[g] = zbout[g]

    sent(lambda q: piece(h, q), (s4, q4))
    sent(lambda q: part(h, q), (s5, q5))

    @pl.loop(1, NBLK)
    def _(d):
        pf = lax.rem(f + d, NBLK)
        hid_copy(stat_s, rstat.at[pf], s3.at[pf], q3.at[pf], sg * NBLK + pf).wait_send()

    @pl.loop(1, n_req)
    def _(d):
        p = lax.rem(g + d, n_req)
        req_copy(zout.at[p], ag.at[h, p], s2.at[p], q2.at[p], p).wait_send()

    @pl.loop(1, n_req)
    def _(d):
        p = lax.rem(g - d + n_req, n_req)
        req_copy(zbin.at[p], zbin.at[p], s6.at[p], q6.at[p], p).wait_recv()

    returned = zbin[...].astype(F32).reshape(pairs, BLK).astype(BF)
    mixture = jnp.dot(weights, returned, preferred_element_type=F32)
    first = jnp.where(sg == 0, 1.0, 0.0)
    rfin[h] = (mixture + stream_wide * first).astype(BF)

    def final(p, q):
        return rfin.at[p, pl.ds(q * rowq1, rowq1)]

    finished = []

    def wait_back(p, c):
        if finished:
            return
        finished.append(True)

        @pl.loop(1, n_req)
        def _(d):
            p = lax.rem(g + d, n_req)
            req_copy(zbout.at[p], zbin.at[p], s6.at[p], q6.at[p], p).wait_send()

    gather_over_hid(final, (s7, q7), lambda q: None, wait_back)

    for b in range(NBLK):
        size = min(BLK, width - b * BLK)
        both = rfin[b].astype(F32) + rfin[NBLK + b].astype(F32)
        out_ref[:, b * BLK : b * BLK + size] = both[:, :size].astype(BF)

    sent(lambda q: final(h, q), (s7, q7))


def ring_buffers(size):
    return [
        pltpu.VMEM((4, 4, size, BLK), BF),
        pltpu.VMEM((4, 4, size, BLK), BF),
        pltpu.VMEM((4, 4, size, BLK), BF),
        pltpu.VMEM((4, 4, 2, size, BLK), BF),
        pltpu.VMEM((4, size, BLK), BF),
        pltpu.VMEM((4, 2, size, BLK), BF),
    ]


def on_device(
    attn_partial,
    residual,
    norm_gain,
    router_weight,
    router_bias,
    routes,
    gate_up,
    gate_up_bias,
    down_weight,
    down_bias,
):
    n_req, n_hid = lax.axis_size("req"), lax.axis_size("hid")
    rows, width = residual.shape
    wide = BLK * NBLK
    per = n_req * SLOTS
    vmem = pl.BlockSpec(memory_space=pltpu.VMEM)
    hbm = pl.BlockSpec(memory_space=pl.ANY)
    dma = pltpu.SemaphoreType.DMA
    hid_sem, req_sem = dma((n_hid,)), dma((n_req,))
    return pl.pallas_call(
        functools.partial(moe_kernel, n_req, n_hid),
        out_shape=jax.ShapeDtypeStruct((rows, width), BF),
        in_specs=[hbm] * 2 + [vmem] * 6 + [hbm] * 2,
        out_specs=vmem,
        scratch_shapes=[
            pltpu.VMEM((rows, width), BF),
            pltpu.VMEM((rows, width), BF),
            pltpu.VMEM((rows, wide), BF),
            pltpu.VMEM((rows, wide), BF),
            pltpu.VMEM((1, wide), F32),
            pltpu.VMEM((128, wide), BF),
            pltpu.VMEM((1, wide), F32),
            pltpu.VMEM(gate_up.shape[:0:-1], BF),
            pltpu.VMEM(down_weight.shape[1:], BF),
            pltpu.VMEM((512, wide), BF),
            pltpu.VMEM((256, wide), BF),
            *ring_buffers(rows // 4),
            pltpu.VMEM((rows, 128), F32),
            pltpu.VMEM((NBLK, rows, 128), F32),
            pltpu.VMEM((n_req, SLOTS, BLK), BF),
            pltpu.VMEM((n_hid, n_req, SLOTS, BLK), BF),
            pltpu.VMEM((2, per, 512), F32),
            pltpu.VMEM((2, per, 128), F32),
            pltpu.VMEM((2, per, 256), BF),
            pltpu.VMEM((n_hid, per, BLK), BF),
            *ring_buffers(per // 4),
            pltpu.VMEM((n_req, SLOTS, BLK), BF),
            pltpu.VMEM((n_req, SLOTS, BLK), BF),
            pltpu.VMEM((n_hid, rows, BLK), BF),
            dma((4,)),
            dma((4, 15)),
            dma((4, 15)),
            req_sem,
            req_sem,
            dma((NBLK,)),
            dma((NBLK,)),
            dma((4, 15)),
            dma((n_hid, 4)),
            dma((4, 15)),
            dma((4, 15)),
            req_sem,
            req_sem,
            dma((4, 15)),
            dma((n_hid, 4)),
        ],
        compiler_params=pltpu.CompilerParams(
            collective_id=0, has_side_effects=True, vmem_limit_bytes=56 * 1024 * 1024
        ),
        name="moe_block",
    )(
        attn_partial[0],
        residual,
        norm_gain,
        router_weight.T,
        router_bias.reshape(1, -1),
        routes.T,
        gate_up_bias,
        down_bias,
        gate_up[0].T,
        down_weight[0],
    )


def solution(mesh):
    return jax.shard_map(
        on_device,
        mesh=mesh,
        in_specs=(
            P("hid", "req", None),
            P("req", None),
            P(),
            P(),
            P(),
            P("req", None),
            P("req", None, "hid"),
            P("req", "hid"),
            P("req", "hid", None),
            P("req", None),
        ),
        out_specs=P("req", None),
        check_vma=False,
    )
```

```python
import functools

import jax
import jax.numpy as jnp
from jax import lax
from jax.experimental import pallas as pl
from jax.experimental.pallas import tpu as pltpu
from jax.sharding import PartitionSpec as P

MESH = pl.DeviceIdType.MESH
BLK = 384
NBLK = 8
SLOTS = 8
BF = jnp.bfloat16
F32 = jnp.float32


def lanes(block):
    return pl.ds(pl.multiple_of(block * BLK, 128), BLK)


def dot_nt(left, right):
    return lax.dot_general(
        left, right, (((1,), (1,)), ((), ())), preferred_element_type=F32
    )


def moe_kernel(
    n_req,
    n_hid,
    attn_hbm,
    resid_hbm,
    gain_ref,
    wr_ref,
    rb_ref,
    routes_ref,
    bgu_ref,
    db_ref,
    wgu_hbm,
    wd_hbm,
    out_ref,
    attn_v,
    resid_v,
    attn_s,
    resid_s,
    gain_s,
    wr_s,
    db_s,
    wgu_v,
    wd_v,
    wg_s,
    wd_s,
    mid1,
    sum1,
    rb1_1,
    rb2_1,
    ra1_1,
    ra2_1,
    stat_s,
    rstat,
    zout,
    ag,
    acc,
    ssq,
    act_s,
    pout,
    mid5,
    sum5,
    rb1,
    rb2,
    ra1,
    ra2,
    zbout,
    zbin,
    rfin,
    w_sem,
    s1,
    q1,
    s2,
    q2,
    s3,
    q3,
    s4,
    q4,
    s5,
    q5,
    s6,
    q6,
    s7,
    q7,
):
    rows, width = attn_hbm.shape
    experts = rb_ref.shape[1]
    half = wd_hbm.shape[0]
    wide = BLK * NBLK
    tail = wide - 256
    h = lax.axis_index("hid")
    g = lax.axis_index("req")
    sg = lax.div(h, NBLK)
    f = lax.rem(h, NBLK)

    get_attn = pltpu.make_async_copy(attn_hbm, attn_v, w_sem.at[2])
    get_resid = pltpu.make_async_copy(resid_hbm, resid_v, w_sem.at[3])
    get_attn.start()
    get_resid.start()
    get_wgu = pltpu.make_async_copy(wgu_hbm, wgu_v, w_sem.at[0])
    get_wd = pltpu.make_async_copy(wd_hbm, wd_v, w_sem.at[1])
    get_wgu.start()
    get_wd.start()

    barrier = pltpu.get_barrier_semaphore()

    @pl.loop(1, n_req)
    def _(i):
        step = lax.div(n_req + 1 - i, 2)
        d = step + lax.rem(n_req + 1 - i, 2) * (n_req - 2 * step)
        pl.semaphore_signal(
            barrier, inc=1, device_id={"req": lax.rem(g + d, n_req)}, device_id_type=MESH
        )

    @pl.loop(1, n_hid)
    def _(d):
        pl.semaphore_signal(
            barrier, inc=1, device_id={"hid": lax.rem(h + d, n_hid)}, device_id_type=MESH
        )

    attn_s[:, tail:] = jnp.zeros((rows, wide - tail), BF)
    get_attn.wait()
    attn_s[:, :width] = attn_v[...]
    resid_s[:, tail:] = jnp.zeros((rows, wide - tail), BF)
    get_resid.wait()
    resid_s[:, :width] = resid_v[...]
    gain_s[:, tail:] = jnp.zeros((1, wide - tail), F32)
    gain_s[:, :width] = gain_ref[...].reshape(1, width).astype(F32)
    db_s[:, tail:] = jnp.zeros((1, wide - tail), F32)
    db_s[:, :width] = db_ref[...].astype(F32)

    pl.semaphore_wait(barrier, n_hid + n_req - 2)

    def hid_copy(src, dst, send, recv, peer):
        return pltpu.make_async_remote_copy(
            src_ref=src,
            dst_ref=dst,
            send_sem=send,
            recv_sem=recv,
            device_id={"hid": peer},
            device_id_type=MESH,
        )

    def req_copy(src, dst, send, recv, peer):
        return pltpu.make_async_remote_copy(
            src_ref=src,
            dst_ref=dst,
            send_sem=send,
            recv_sem=recv,
            device_id={"req": peer},
            device_id_type=MESH,
        )

    side = 4
    x = lax.div(h, side)
    y = lax.rem(h, side)

    def at(c, da, db):
        a = lax.rem((x if c == 0 else y) + da, side)
        b = lax.rem((y if c == 0 else x) + db, side)
        return a * side + b if c == 0 else b * side + a

    def order(n, q):
        return (q // 2, q % 2) if n == 4 else (q, q)

    def scatter_first(n, src, bufs, sems, make):
        rb1 = bufs[2]
        rb2 = bufs[3]

        def send(q, k, ref, dst, peer):
            hid_copy(ref, dst, sems[0].at[q, k], sems[1].at[q, k], peer).start()

        @pl.loop(0, 4)
        def _(j):
            for c in range(2):
                make(at(c, j, 2), c)
            for q in range(n):
                c, odd = order(n, q)
                peer = at(c, 0, 1) if odd else at(c, 0, 3)
                send(q, j, src(at(c, j, 2), q), rb1.at[q, j], peer)

        @pl.loop(0, 4)
        def _(j):
            for c in range(2):
                make(at(c, j, 1), c)
                make(at(c, j, 3), c)
            for q in range(n):
                c, odd = order(n, q)
                to = 3 if odd else 1
                send(q, 4 + j, src(at(c, j, to), q), rb2.at[q, j, 0], at(c, 0, to))

    def scatter_rest(n, src, bufs, sems, make):
        mid, sums, rb1, rb2, ra1, ra2 = bufs

        def send(q, k, ref, dst, peer):
            hid_copy(ref, dst, sems[0].at[q, k], sems[1].at[q, k], peer).start()

        def landed(q, k, dst):
            hid_copy(dst, dst, sems[0].at[q, 0], sems[1].at[q, k], at(0, 1, 0)).wait_recv()

        @pl.loop(0, 4)
        def _(j):
            for q in range(n):
                c, odd = order(n, q)
                to = 1 if odd else 3
                landed(q, j, rb1.at[q, j])
                both = src(at(c, j, to), q)[...].astype(F32) + rb1[q, j].astype(F32)
                mid[q, j] = both.astype(BF)
                send(q, 8 + j, mid.at[q, j], rb2.at[q, j, 1], at(c, 0, to))
            for c in range(2):
                make(at(c, j, 0), c)

        def line_sum(j, q):
            landed(q, 4 + j, rb2.at[q, j, 0])
            landed(q, 8 + j, rb2.at[q, j, 1])
            three = src(at(order(n, q)[0], j, 0), q)[...].astype(F32)
            return three + rb2[q, j, 0].astype(F32) + rb2[q, j, 1].astype(F32)

        for q in range(n):
            c, odd = order(n, q)
            sums[q, 2] = line_sum(2, q).astype(BF)
            send(q, 12, sums.at[q, 2], ra1.at[q], at(c, 1 if odd else 3, 0))
        for q in range(n):
            c, odd = order(n, q)
            to = 3 if odd else 1
            sums[q, to] = line_sum(to, q).astype(BF)
            send(q, 13, sums.at[q, to], ra2.at[q, 0], at(c, to, 0))
        for q in range(n):
            c, odd = order(n, q)
            to = 1 if odd else 3
            near = line_sum(to, q)
            landed(q, 12, ra1.at[q])
            sums[q, to] = (near + ra1[q].astype(F32)).astype(BF)
            send(q, 14, sums.at[q, to], ra2.at[q, 1], at(c, to, 0))

        def result(q):
            total = line_sum(0, q)
            landed(q, 13, ra2.at[q, 0])
            landed(q, 14, ra2.at[q, 1])
            return total + ra2[q, 0].astype(F32) + ra2[q, 1].astype(F32)

        return result

    def gather_over_hid(n, piece, sems, ready, after):
        def ship(q, k, p, peer):
            ref = piece(p, q)
            hid_copy(ref, ref, sems[0].at[q, k], sems[1].at[p, q], peer).start()

        def arrive(q, p):
            ref = piece(p, q)
            hid_copy(ref, ref, sems[0].at[q, 0], sems[1].at[p, q], p).wait_recv()

        for q in range(n):
            c, _odd = order(n, q)
            ready(q)
            ship(q, 0, h, at(c, 1, 0))
            ship(q, 1, h, at(c, 3, 0))
            ship(q, 3, h, at(c, 0, 1))
            ship(q, 4, h, at(c, 0, 3))
        for c in range(2):
            after(h, c)
        for q in range(n):
            c, odd = order(n, q)
            arrive(q, at(c, 1, 0))
            arrive(q, at(c, 3, 0))
            if odd:
                ship(q, 2, at(c, 1, 0), at(c, 3, 0))
            else:
                ship(q, 2, at(c, 3, 0), at(c, 1, 0))
            for j in (1, 3):
                ship(q, 3 + 2 * j, at(c, j, 0), at(c, 0, 1))
                ship(q, 4 + 2 * j, at(c, j, 0), at(c, 0, 3))
        for c in range(2):

            @pl.loop(0, 2)
            def _(i):
                after(at(c, 2 * i + 1, 0), c)

        for q in range(n):
            c, _odd = order(n, q)
            arrive(q, at(c, 2, 0))
            ship(q, 7, at(c, 2, 0), at(c, 0, 1))
            ship(q, 8, at(c, 2, 0), at(c, 0, 3))

        @pl.loop(0, 4)
        def _(i):
            j = lax.rem(i + i + i, 4)
            for q in range(n):
                c, odd = order(n, q)
                arrive(q, at(c, j, 1))
                arrive(q, at(c, j, 3))
                if odd:
                    ship(q, 11 + j, at(c, j, 1), at(c, 0, 3))
                else:
                    ship(q, 11 + j, at(c, j, 3), at(c, 0, 1))

        for c in range(2):
            after(at(c, 2, 0), c)

            @pl.loop(0, 4)
            def _(j):
                after(at(c, j, 1), c)
                after(at(c, j, 3), c)

        @pl.loop(0, 4)
        def _(i):
            j = lax.rem(i + i + i, 4)
            for q in range(n):
                arrive(q, at(order(n, q)[0], j, 2))
            for c in range(2):
                after(at(c, j, 2), c)

    def sent(n, refs, sems):
        for q in range(n):

            @pl.loop(0, 15)
            def _(k):
                ref = refs(q)
                hid_copy(ref, ref, sems[0].at[q, k], sems[0].at[q, k], at(0, 1, 0)).wait_send()

    def nothing(p, c):
        pass

    bufs1 = (mid1, sum1, rb1_1, rb2_1, ra1_1, ra2_1)
    rowq1 = rows // 2

    def share(p, q):
        return attn_s.at[pl.ds(q * rowq1, rowq1), lanes(lax.rem(p, NBLK))]

    scatter_first(2, share, bufs1, (s1, q1), nothing)

    wr_s[...] = jnp.zeros(wr_s.shape, BF)
    wr_s[0:experts, 0:width] = wr_ref[...]
    named = lax.broadcasted_iota(jnp.int32, (experts, rows), 0)
    mask_t = jnp.zeros((experts, rows), F32)
    for k in range(routes_ref.shape[0]):
        mask_t = mask_t + jnp.where(routes_ref[k : k + 1, :] == named, 1.0, 0.0)
    row_a = lax.broadcasted_iota(jnp.int32, (rows, rows), 0)
    row_b = lax.broadcasted_iota(jnp.int32, (rows, rows), 1)
    same = (row_a == row_b).astype(BF)
    mask_t = mask_t.astype(BF)
    slot_t = jnp.dot(mask_t, (row_a < row_b).astype(BF), preferred_element_type=F32)
    pairs = experts * SLOTS
    col = lax.broadcasted_iota(jnp.int32, (pairs, experts), 0)
    own = lax.broadcasted_iota(jnp.int32, (pairs, experts), 1)
    expand_t = (lax.div(col, SLOTS) == own).astype(BF)
    slot_wide = jnp.dot(expand_t, slot_t.astype(BF), preferred_element_type=F32)
    mask_wide = jnp.dot(expand_t, mask_t, preferred_element_type=F32)
    want = lax.rem(lax.broadcasted_iota(jnp.int32, (pairs, rows), 0), SLOTS) + sg * SLOTS
    chosen_t = jnp.where((slot_wide == want.astype(F32)) & (mask_wide > 0.5), 1.0, 0.0)
    chosen_t = chosen_t.astype(BF)
    chosen = dot_nt(same, chosen_t)
    mask = dot_nt(same, mask_t)

    result1 = scatter_rest(2, share, bufs1, (s1, q1), nothing)
    attention = jnp.concatenate([result1(q) for q in range(2)], axis=0)
    stream = (resid_s[:, lanes(f)].astype(F32) + attention).astype(BF)
    stream_wide = stream.astype(F32)

    picked = jnp.dot(chosen_t, stream, preferred_element_type=F32)
    zout[...] = picked.reshape(experts, SLOTS, BLK).astype(BF)

    @pl.loop(1, n_req)
    def _(i):
        step = lax.div(i + 1, 2)
        d = step + lax.rem(i + 1, 2) * (n_req - 2 * step)
        p = lax.rem(g + d, n_req)
        req_copy(zout.at[p], ag.at[h, g], s2.at[p], q2.at[g], p).start()

    scaled = (stream_wide * gain_s[:, lanes(f)]).astype(BF)
    stats = dot_nt(scaled, wr_s[:, lanes(f)])
    squares = jnp.sum(stream_wide * stream_wide, axis=1, keepdims=True)
    lane = lax.broadcasted_iota(jnp.int32, (rows, 128), 1)
    stat_s[...] = jnp.where(lane == experts, squares, stats)

    @pl.loop(1, NBLK)
    def _(d):
        pf = lax.rem(f + d, NBLK)
        hid_copy(
            stat_s, rstat.at[f], s3.at[pf], q3.at[f], sg * NBLK + pf
        ).start()

    get_wgu.wait()
    twice = wgu_v.shape[0]
    from_col = lax.broadcasted_iota(jnp.int32, (512, twice), 1)
    to_col = lax.broadcasted_iota(jnp.int32, (512, twice), 0)
    perm = (to_col == lax.rem(from_col, 2) * 256 + lax.div(from_col, 2)).astype(BF)
    wg_s[:, tail:] = jnp.zeros((512, wide - tail), BF)

    @pl.loop(0, width // BLK)
    def _(i):
        at = lanes(i)
        wg_s[:, at] = jnp.dot(perm, wgu_v[:, at], preferred_element_type=F32).astype(BF)

    last = width // BLK * BLK
    wg_s[:, last:width] = jnp.dot(
        perm, wgu_v[:, last:width], preferred_element_type=F32
    ).astype(BF)
    bias = dot_nt(jnp.broadcast_to(bgu_ref[...], (16, twice)), perm)[0:1, :]
    get_wd.wait()
    wd_s[...] = jnp.zeros(wd_s.shape, BF)
    wd_s[0:half, 0:width] = wd_v[...]
    acc[...] = jnp.zeros(acc.shape, F32)
    ssq[...] = jnp.zeros(ssq.shape, F32)

    quart = n_req // 4
    half0 = lax.div(g, 2 * quart)

    def group_at(q):
        return lax.rem(half0 + q // 2, 2) * (2 * quart) + q % 2 * quart

    def piece(p, q):
        return ag.at[p, pl.ds(group_at(q), quart)]

    def use_half(p, c):
        first = group_at(2 * c)
        wide_rows = ag[p, pl.ds(first, 2 * quart)].astype(F32)
        count = 2 * quart * SLOTS
        wide_rows = wide_rows.reshape(count, BLK)
        to = lax.div(p, NBLK)
        blk = lax.rem(p, NBLK)
        sq = wide_rows * wide_rows
        here = pl.ds(pl.multiple_of(first * SLOTS, count), count)
        ssq[to, here] += sq[:, 0:128] + sq[:, 128:256] + sq[:, 256:384]
        u = (wide_rows * gain_s[:, lanes(blk)]).astype(BF)
        acc[to, here] += dot_nt(u, wg_s[:, lanes(blk)])

    def arrived(q):
        @pl.loop(0, quart)
        def _(i):
            p = group_at(q) + i

            @pl.when(p != g)
            def _():
                req_copy(zout.at[p], ag.at[h, p], s2.at[p], q2.at[p], p).wait_recv()

    sent(2, lambda q: share(h, q), (s1, q1))
    ag[h, g] = zout[g]
    gather_over_hid(4, piece, (s4, q4), arrived, use_half)

    for side_at in range(2):
        mean = jnp.sum(ssq[side_at], axis=1, keepdims=True) * (1.0 / width)
        inverse = lax.rsqrt(mean + 1e-05)
        gate = jnp.minimum(acc[side_at, :, 0:256] * inverse + bias[:, 0:256], 7.0)
        up = jnp.clip(acc[side_at, :, 256:512] * inverse + bias[:, 256:512], -7.0, 7.0)
        act_s[side_at] = ((up + 1.0) * gate * jax.nn.sigmoid(1.702 * gate)).astype(BF)

    rowq = quart * SLOTS

    def down(p, c):
        here = slice(c * 2 * rowq, (c + 1) * 2 * rowq)
        pout[p, here] = jnp.dot(
            act_s[lax.div(p, NBLK), here],
            wd_s[:, lanes(lax.rem(p, NBLK))],
            preferred_element_type=F32,
        ).astype(BF)

    def part(p, q):
        return pout.at[p, pl.ds(q * rowq, rowq)]

    bufs5 = (mid5, sum5, rb1, rb2, ra1, ra2)
    scatter_first(4, part, bufs5, (s5, q5), down)
    total_stats = stat_s[...]
    for d in range(1, NBLK):
        pf = lax.rem(f - d + NBLK, NBLK)
        hid_copy(rstat.at[pf], rstat.at[pf], s3.at[pf], q3.at[pf], sg * NBLK + pf).wait_recv()
        total_stats = total_stats + rstat[pf]
    row_sq = jnp.sum(jnp.where(lane == experts, total_stats, 0.0), axis=1, keepdims=True)
    row_inverse = lax.rsqrt(row_sq * (1.0 / width) + 1e-05)
    logits = total_stats[:, 0:experts] * row_inverse + rb_ref[...]
    raised = jnp.where(mask > 0.5, jnp.exp(jnp.where(mask > 0.5, logits, 0.0)), 0.0)
    combine = (raised / jnp.sum(raised, axis=1, keepdims=True)).astype(BF)
    combine_wide = dot_nt(combine, expand_t)
    weights = jnp.where(chosen > 0.5, combine_wide, 0.0).astype(BF)

    result5 = scatter_rest(4, part, bufs5, (s5, q5), down)

    for q in range(4):
        expert_out = result5(q) + db_s[:, lanes(f)]
        zbout[q * quart : (q + 1) * quart] = expert_out.reshape(quart, SLOTS, BLK).astype(BF)

        @pl.loop(q * quart, (q + 1) * quart)
        def _(p):
            @pl.when(p != g)
            def _():
                req_copy(zbout.at[p], zbin.at[g], s6.at[p], q6.at[g], p).start()

    zbin[g] = zbout[g]

    sent(4, lambda q: piece(h, q), (s4, q4))
    sent(4, lambda q: part(h, q), (s5, q5))

    @pl.loop(1, NBLK)
    def _(d):
        pf = lax.rem(f + d, NBLK)
        hid_copy(stat_s, rstat.at[pf], s3.at[pf], q3.at[pf], sg * NBLK + pf).wait_send()

    @pl.loop(1, n_req)
    def _(d):
        p = lax.rem(g + d, n_req)
        req_copy(zout.at[p], ag.at[h, p], s2.at[p], q2.at[p], p).wait_send()

    @pl.loop(1, n_req)
    def _(d):
        p = lax.rem(g - d + n_req, n_req)
        req_copy(zbin.at[p], zbin.at[p], s6.at[p], q6.at[p], p).wait_recv()

    returned = zbin[...].astype(F32).reshape(pairs, BLK).astype(BF)
    mixture = jnp.dot(weights, returned, preferred_element_type=F32)
    first = jnp.where(sg == 0, 1.0, 0.0)
    rfin[h] = (mixture + stream_wide * first).astype(BF)

    def final(p, q):
        return rfin.at[p, pl.ds(q * rowq1, rowq1)]

    finished = []

    def wait_back(p, c):
        if finished:
            return
        finished.append(True)

        @pl.loop(1, n_req)
        def _(d):
            p = lax.rem(g + d, n_req)
            req_copy(zbout.at[p], zbin.at[p], s6.at[p], q6.at[p], p).wait_send()

    gather_over_hid(2, final, (s7, q7), lambda q: None, wait_back)

    for b in range(NBLK):
        size = min(BLK, width - b * BLK)
        both = rfin[b].astype(F32) + rfin[NBLK + b].astype(F32)
        out_ref[:, b * BLK : b * BLK + size] = both[:, :size].astype(BF)

    sent(2, lambda q: final(h, q), (s7, q7))


def ring_buffers(n, size):
    return [
        pltpu.VMEM((n, 4, size, BLK), BF),
        pltpu.VMEM((n, 4, size, BLK), BF),
        pltpu.VMEM((n, 4, size, BLK), BF),
        pltpu.VMEM((n, 4, 2, size, BLK), BF),
        pltpu.VMEM((n, size, BLK), BF),
        pltpu.VMEM((n, 2, size, BLK), BF),
    ]


def on_device(
    attn_partial,
    residual,
    norm_gain,
    router_weight,
    router_bias,
    routes,
    gate_up,
    gate_up_bias,
    down_weight,
    down_bias,
):
    n_req, n_hid = lax.axis_size("req"), lax.axis_size("hid")
    rows, width = residual.shape
    wide = BLK * NBLK
    per = n_req * SLOTS
    vmem = pl.BlockSpec(memory_space=pltpu.VMEM)
    hbm = pl.BlockSpec(memory_space=pl.ANY)
    dma = pltpu.SemaphoreType.DMA
    hid_sem, req_sem = dma((n_hid,)), dma((n_req,))
    return pl.pallas_call(
        functools.partial(moe_kernel, n_req, n_hid),
        out_shape=jax.ShapeDtypeStruct((rows, width), BF),
        in_specs=[hbm] * 2 + [vmem] * 6 + [hbm] * 2,
        out_specs=vmem,
        scratch_shapes=[
            pltpu.VMEM((rows, width), BF),
            pltpu.VMEM((rows, width), BF),
            pltpu.VMEM((rows, wide), BF),
            pltpu.VMEM((rows, wide), BF),
            pltpu.VMEM((1, wide), F32),
            pltpu.VMEM((128, wide), BF),
            pltpu.VMEM((1, wide), F32),
            pltpu.VMEM(gate_up.shape[:0:-1], BF),
            pltpu.VMEM(down_weight.shape[1:], BF),
            pltpu.VMEM((512, wide), BF),
            pltpu.VMEM((256, wide), BF),
            *ring_buffers(2, rows // 2),
            pltpu.VMEM((rows, 128), F32),
            pltpu.VMEM((NBLK, rows, 128), F32),
            pltpu.VMEM((n_req, SLOTS, BLK), BF),
            pltpu.VMEM((n_hid, n_req, SLOTS, BLK), BF),
            pltpu.VMEM((2, per, 512), F32),
            pltpu.VMEM((2, per, 128), F32),
            pltpu.VMEM((2, per, 256), BF),
            pltpu.VMEM((n_hid, per, BLK), BF),
            *ring_buffers(4, per // 4),
            pltpu.VMEM((n_req, SLOTS, BLK), BF),
            pltpu.VMEM((n_req, SLOTS, BLK), BF),
            pltpu.VMEM((n_hid, rows, BLK), BF),
            dma((4,)),
            dma((4, 15)),
            dma((4, 15)),
            req_sem,
            req_sem,
            dma((NBLK,)),
            dma((NBLK,)),
            dma((4, 15)),
            dma((n_hid, 4)),
            dma((4, 15)),
            dma((4, 15)),
            req_sem,
            req_sem,
            dma((4, 15)),
            dma((n_hid, 4)),
        ],
        compiler_params=pltpu.CompilerParams(
            collective_id=0, has_side_effects=True, vmem_limit_bytes=56 * 1024 * 1024
        ),
        name="moe_block",
    )(
        attn_partial[0],
        residual,
        norm_gain,
        router_weight.T,
        router_bias.reshape(1, -1),
        routes.T,
        gate_up_bias,
        down_bias,
        gate_up[0].T,
        down_weight[0],
    )


def solution(mesh):
    return jax.shard_map(
        on_device,
        mesh=mesh,
        in_specs=(
            P("hid", "req", None),
            P("req", None),
            P(),
            P(),
            P(),
            P("req", None),
            P("req", None, "hid"),
            P("req", "hid"),
            P("req", "hid", None),
            P("req", None),
        ),
        out_specs=P("req", None),
        check_vma=False,
    )
```
